128 devices in a mesh: seq: 16 (over z, y), head: 8 (over x, core).
Axes of the slice: x: 4, y: 4, z: 4, core: 2. Of those that a mesh axis runs over, the one named last changes fastest.
Arguments:
- queries: bfloat16 [16384, 4096], P(('seq', 'head')), may hold values from -52 to 52
- keys: bfloat16 [16384, 4096], P(('seq', 'head')), may hold values from -4 to 4
- values: bfloat16 [16384, 4096], P(('seq', 'head')), may hold values from -32 to 32
- grad_out: bfloat16 [16384, 4096], P(('seq', 'head')), may hold values from -64 to 64
- rand_blocks: int32 [32, 256, 3], P('head', 'seq'), may hold values from 0 to 255, as said below
- global_ids: int32 [2], replicated, may hold values from 0 to 255
- drop_mask: int32 [32, 256, 8], P('head', 'seq'), may hold values 0 or 1
Outputs:
- attended: bfloat16 [16384, 4096], P('seq', 'head')
- grad_queries: bfloat16 [16384, 4096], P('seq', 'head')
- grad_keys: bfloat16 [16384, 4096], P('seq', 'head')
- grad_values: bfloat16 [16384, 4096], P('seq', 'head')
The draws below stay inside these ranges and needn't reach their ends.
Inputs may be any that keep to these rules, and one draw needn't show every extreme that they name: `rand_blocks`: for every sequence shard s (query blocks s * 16 onward) and head group g (heads g * 4 onward), the 192 listed random blocks come from a g-dependent hot shard exactly 15 times, and from no shard more than 15 times; the rest spread evenly over the other shards; the hot shard is the same for all s of one head group.
All inputs are finite; a program needn't handle non-finite values. No bound on the sum of `drop_mask` on one device may be relied on, other than what follows from the above.
Results may differ from the reference program's by a relative error of at most 0.015.
Values may be sent and summed in bfloat16 or wider, within the bound.
A program may use at most 128 MiB of HBM per device.

```python
import jax
import jax.numpy as jnp
from jax import lax

D = 4096
H = 32
HEAD_WIDTH = 128
BLOCK_TOKENS = 64
R = 3
G = 2
SEQ_LEN = 16384
SEQUENCE_BLOCKS = 256
NBD = 16
HD = 4
KEY_BLOCKS = 8
REQ = 192
CAP = 15


def query_key_pair(key):
    key_seed = jax.random.fold_in(key, 11)
    query_seed = jax.random.fold_in(key, 12)
    shape = (SEQ_LEN, D)
    key_rows = jax.random.truncated_normal(key_seed, -4.0, 4.0, shape, jnp.float32)
    query_lines = jax.random.truncated_normal(query_seed, -4.0, 4.0, shape, jnp.float32)
    return (key_rows, query_lines)


def draw_queries(key, part):
    return query_key_pair(key)[1].astype(jnp.bfloat16)


def draw_keys(key, part):
    return query_key_pair(key)[0].astype(jnp.bfloat16)


def draw_rand_blocks(key, part):
    shard_count = SEQUENCE_BLOCKS // NBD
    group_count = H // HD
    hottest = jax.random.randint(jax.random.fold_in(key, 21), (group_count,), 0, shard_count)
    position = jnp.arange(REQ)
    others = (hottest[None, :, None] + 1 + (position[None, None, :] - CAP) % (shard_count - 1)) % shard_count
    labels = jnp.where(position[None, None, :] < CAP, hottest[None, :, None], others)
    labels = jnp.broadcast_to(labels, (shard_count, group_count, REQ))
    noise = jax.random.randint(jax.random.fold_in(key, 22), (shard_count, group_count, REQ), 0, 2 ** 20)
    order = jnp.argsort(noise * REQ + position[None, None, :], axis=-1, stable=True)
    labels = jnp.take_along_axis(labels, order, axis=-1)
    inside = jax.random.randint(jax.random.fold_in(key, 23), (shard_count, group_count, REQ), 0, NBD)
    chosen = labels * NBD + inside
    chosen = chosen.reshape(shard_count, group_count, HD, NBD, R).transpose(1, 2, 0, 3, 4)
    return chosen.reshape(H, SEQUENCE_BLOCKS, R).astype(jnp.int32)


def with_ends(entries, stream_key, smallest, top_value):
    place = [jax.random.randint(jax.random.fold_in(stream_key, axis), (), 0, length) for axis, length in enumerate(entries.shape)]
    widest = entries.shape.index(max(entries.shape))
    neighbour = place[:widest] + [(place[widest] + 1) % entries.shape[widest]] + place[widest + 1:]
    return entries.at[tuple(place)].set(smallest).at[tuple(neighbour)].set(top_value)


def level_of(own_key, shape, cuts, least, top_value):
    loudness, own = 1.0, jax.random.fold_in(own_key, 6)
    for axis_at, parts in cuts:
        steps = jnp.exp(jax.random.uniform(jax.random.fold_in(own, axis_at), (parts,), jnp.float32, least / len(cuts), top_value / len(cuts)))
        loudness = loudness * jnp.repeat(steps, shape[axis_at] // parts).reshape([-1 if axis == axis_at else 1 for axis in range(len(shape))])
    return loudness


def bell_draw(key, extent, scale, reach, shards=(), held_as=jnp.bfloat16):
    array = scale * jax.random.normal(key, extent, jnp.float32)
    if shards:
        array = array * level_of(key, extent, shards, -0.22, 0.18)
    return jnp.clip(array, -reach, reach).astype(held_as)


def setup_inputs(seed: int = 0) -> dict:
    splits = jax.random.split(jax.random.key(seed), 8)
    queries = draw_queries(jax.random.fold_in(splits[7], 71), 0)
    keys = draw_keys(jax.random.fold_in(splits[7], 71), 0)
    values = bell_draw(splits[2], (SEQ_LEN, D), 6.0, 32.0, ((0, 128),))
    grad_out = bell_draw(splits[3], (SEQ_LEN, D), 12.0, 64.0, ((0, 128),))
    rand_blocks = draw_rand_blocks(jax.random.fold_in(splits[7], 71), 0)
    global_ids = jax.random.randint(splits[5], (G,), 0, SEQUENCE_BLOCKS).astype(jnp.int32)
    drop_mask = with_ends((jax.random.randint(splits[6], (H, SEQUENCE_BLOCKS, KEY_BLOCKS), 0, 10) < 9).astype(jnp.int32), jax.random.fold_in(splits[6], 1), 0, 1)
    return {"queries": queries, "keys": keys, "values": values, "grad_out": grad_out, "rand_blocks": rand_blocks, "global_ids": global_ids, "drop_mask": drop_mask}


keep_prob = 0.9


def head_major(tensor):
    return tensor.reshape(SEQUENCE_BLOCKS, BLOCK_TOKENS, H, HEAD_WIDTH).transpose(2, 0, 1, 3)


def token_major(tensor):
    return tensor.transpose(1, 2, 0, 3).reshape(SEQ_LEN, D)


def reference(queries, keys, values, grad_out, rand_blocks, global_ids, drop_mask):
    logit_scale = HEAD_WIDTH ** -0.5
    blocks = jnp.arange(SEQUENCE_BLOCKS, dtype=jnp.int32)
    window = jnp.stack([blocks - 1, blocks, blocks + 1], axis=1)
    globals_listed = jnp.broadcast_to(global_ids.astype(jnp.int32)[None, :], (SEQUENCE_BLOCKS, G))
    present = jnp.concatenate([(blocks >= 1)[:, None], jnp.ones((SEQUENCE_BLOCKS, 1), bool), (blocks <= SEQUENCE_BLOCKS - 2)[:, None], jnp.ones((SEQUENCE_BLOCKS, G + R), bool)], axis=1)
    wide_present = jnp.repeat(present, BLOCK_TOKENS, axis=1)[:, None, :]

    def one_head(inputs):
        query_lines, key_rows, value_rows, gradient_rows, random_ids, drop_bits = inputs
        key_lists = jnp.concatenate([window, globals_listed, random_ids.astype(jnp.int32)], axis=1)
        safe_ids = jnp.clip(key_lists, 0, SEQUENCE_BLOCKS - 1).astype(jnp.int32)
        every_key = key_rows[safe_ids].reshape(SEQUENCE_BLOCKS, KEY_BLOCKS * BLOCK_TOKENS, HEAD_WIDTH).astype(jnp.float32)
        every_value = value_rows[safe_ids].reshape(SEQUENCE_BLOCKS, KEY_BLOCKS * BLOCK_TOKENS, HEAD_WIDTH).astype(jnp.float32)
        query_float = query_lines.astype(jnp.float32)
        float_gradient = gradient_rows.astype(jnp.float32)
        attention_logits = jnp.einsum('ran,rln->ral', query_float, every_key) * logit_scale
        attention_logits = jnp.where(wide_present, attention_logits, -jnp.inf)
        top = jnp.max(attention_logits, axis=-1, keepdims=True)
        expd = jnp.exp(attention_logits - top)
        probs = expd / jnp.sum(expd, axis=-1, keepdims=True)
        retain_scale = jnp.repeat(drop_bits.astype(jnp.float32) / keep_prob, BLOCK_TOKENS, axis=1)[:, None, :]
        after_dropout = (probs * retain_scale).astype(jnp.bfloat16).astype(jnp.float32)
        attended = jnp.einsum('ymn,ynh->ymh', after_dropout, every_value).astype(jnp.bfloat16)
        probability_grad = jnp.einsum('ran,rln->ral', float_gradient, every_value) * retain_scale
        delta = jnp.sum(probs * probability_grad, axis=-1, keepdims=True)
        score_grad = (probs * (probability_grad - delta)).astype(jnp.bfloat16).astype(jnp.float32)
        query_gradient = (jnp.einsum('ymn,ynh->ymh', score_grad, every_key) * logit_scale).astype(jnp.bfloat16)
        key_pieces = (jnp.einsum('efu,efy->euy', score_grad, query_float) * logit_scale).reshape(SEQUENCE_BLOCKS, KEY_BLOCKS, BLOCK_TOKENS, HEAD_WIDTH)
        value_pieces = jnp.einsum('efu,efy->euy', after_dropout, float_gradient).reshape(SEQUENCE_BLOCKS, KEY_BLOCKS, BLOCK_TOKENS, HEAD_WIDTH)
        split_position = 3 + G
        rounded_k = lax.optimization_barrier(key_pieces[:, split_position:].astype(jnp.bfloat16)).astype(jnp.float32)
        rounded_v = lax.optimization_barrier(value_pieces[:, split_position:].astype(jnp.bfloat16)).astype(jnp.float32)
        key_pieces = jnp.concatenate([key_pieces[:, :split_position], rounded_k], axis=1)
        value_pieces = jnp.concatenate([value_pieces[:, :split_position], rounded_v], axis=1)
        grad_k = jnp.zeros((SEQUENCE_BLOCKS, BLOCK_TOKENS, HEAD_WIDTH), jnp.float32).at[safe_ids].add(key_pieces)
        grad_v = jnp.zeros((SEQUENCE_BLOCKS, BLOCK_TOKENS, HEAD_WIDTH), jnp.float32).at[safe_ids].add(value_pieces)
        return attended, query_gradient, grad_k.astype(jnp.bfloat16), grad_v.astype(jnp.bfloat16)

    results = lax.map(one_head, (head_major(queries), head_major(keys), head_major(values), head_major(grad_out), rand_blocks, drop_mask))
    return (token_major(results[0]), token_major(results[1]), token_major(results[2]), token_major(results[3]))
```

```python
import functools
import math

import jax
import jax.numpy as jnp
from jax import lax
from jax.experimental import pallas as pl
from jax.experimental.pallas import tpu as pltpu
from jax.sharding import PartitionSpec as P

W = 128
B = 64
R = 3
G = 2
NS = 16
NH = 8
HD = 4
NB = 16
CAP = 15
REQ = HD * NB * R
T = NB * B
KEEP = 0.9
SCALE = W**-0.5
LOG2E = math.log2(math.e)
MESH = pl.DeviceIdType.MESH
VM = pltpu.VMEM
ANY = pl.ANY
VLIM = 62 * 1024 * 1024

OFFS = (
    (0, 1), (1, 0), (0, 3), (3, 0), (0, 2), (2, 0), (1, 1), (3, 3),
    (1, 3), (3, 1), (1, 2), (2, 1), (3, 2), (2, 3), (2, 2),
)


def seq_peer(s, off):
    return ((s // 4 + off[0]) % 4) * 4 + (s % 4 + off[1]) % 4


def spec(space):
    return pl.BlockSpec(memory_space=space)


def table_kernel(ids_ref, table_ref, slot_ref, count):
    def clear(i, c):
        for o in range(NS):
            table_ref[o, 0, i] = -1
        return c

    lax.fori_loop(0, CAP, clear, 0)
    for o in range(NS):
        count[o] = 0

    def one(i, c):
        block = ids_ref[i]
        owner = block // NB
        rank = count[owner]
        count[owner] = rank + 1
        table_ref[owner, 0, rank] = (i // (NB * R)) * NB + block % NB
        slot_ref[i] = owner * CAP + rank
        return c

    lax.fori_loop(0, REQ, one, 0)


def request_table(ids):
    return pl.pallas_call(
        table_kernel,
        name="request_table",
        out_shape=(
            jax.ShapeDtypeStruct((NS, 1, 128), jnp.int32),
            jax.ShapeDtypeStruct((REQ,), jnp.int32),
        ),
        in_specs=[spec(pltpu.SMEM)],
        out_specs=(spec(pltpu.SMEM), spec(pltpu.SMEM)),
        scratch_shapes=[pltpu.SMEM((NS,), jnp.int32)],
    )(ids)


def fetch_kernel(
    q_in, k_in, v_in, g_in, table, gids,
    q_out, g_out, k_out, v_out, rand_out, glob_out, wanted_out,
    kx, vx, stage, wanted_v, wanted_s, cand, cand_in, chosen,
    send_x, recv_kv, recv_qg, send_t, recv_t, local, send_r, recv_r, halo_s, halo_r, gl_s, gl_r,
):
    s = lax.axis_index("seq")
    hd = lax.axis_index("head")
    barrier = pltpu.get_barrier_semaphore()
    for off in OFFS:
        pl.semaphore_signal(barrier, inc=1, device_id=(seq_peer(s, off), hd), device_id_type=MESH)
    for dh in range(1, NH):
        pl.semaphore_signal(barrier, inc=1, device_id=(s, (hd + dh) % NH), device_id_type=MESH)
    pl.semaphore_wait(barrier, NS - 1 + NH - 1)

    for off in OFFS:
        p = seq_peer(s, off)
        pltpu.make_async_remote_copy(
            table.at[p], wanted_v.at[s], send_t, recv_t, device_id=(p, hd), device_id_type=MESH
        ).start()
    pltpu.make_async_copy(table.at[s], wanted_v.at[s], recv_t).start()

    def x_copy(src, dst, dh, h, rsem):
        p = (hd + dh) % NH
        return pltpu.make_async_remote_copy(
            src.at[:, pl.ds(pl.multiple_of((p * HD + h) * W, W), W)],
            dst.at[pl.ds(pl.multiple_of(h * T + hd * 128, 128), 128), :],
            send_x,
            rsem,
            device_id=(s, p),
            device_id_type=MESH,
        )

    def x_local(src, dst, h, rsem):
        return pltpu.make_async_copy(
            src.at[:, pl.ds(pl.multiple_of((hd * HD + h) * W, W), W)],
            dst.at[pl.ds(pl.multiple_of(h * T + hd * 128, 128), 128), :],
            rsem,
        )

    def tile_pair(src, dst, p, h, i):
        return (
            src.at[pl.ds(i * B, B), pl.ds(pl.multiple_of((p * HD + h) * W, W), W)],
            dst.at[h * NB + hd * 2 + i],
        )

    for h in range(HD):
        for n, (src, dst) in enumerate(((k_in, kx), (v_in, vx))):
            for i in range(2):
                for dh in (1, 6, 7, 2, 3, 4, 5):
                    p = (hd + dh) % NH
                    a, b = tile_pair(src, dst, p, h, i)
                    pltpu.make_async_remote_copy(
                        a, b, send_x, recv_kv.at[n], device_id=(s, p), device_id_type=MESH
                    ).start()
                a, b = tile_pair(src, dst, hd, h, i)
                pltpu.make_async_copy(a, b, recv_kv.at[n]).start()

    pltpu.make_async_copy(wanted_v, wanted_v, recv_t).wait()
    to_smem = pltpu.make_async_copy(wanted_v, wanted_s, local.at[0])
    to_smem.start()
    to_out = pltpu.make_async_copy(wanted_v, wanted_out, local.at[1])
    to_out.start()
    to_smem.wait()

    pltpu.make_async_copy(kx, kx, recv_kv.at[0]).wait()
    pltpu.make_async_copy(vx, vx, recv_kv.at[1]).wait()

    nxt = (s + 1) % NS
    prv = (s + NS - 1) % NS
    for i, (src, dst) in enumerate(((kx, k_out), (vx, v_out))):
        for h in range(HD):
            pltpu.make_async_remote_copy(
                src.at[h * NB + NB - 1], dst.at[h, 0],
                halo_s, halo_r, device_id=(nxt, hd), device_id_type=MESH,
            ).start()
            pltpu.make_async_remote_copy(
                src.at[h * NB], dst.at[h, NB + 1],
                halo_s, halo_r, device_id=(prv, hd), device_id_type=MESH,
            ).start()

    for gb in range(G):
        mine = jnp.clip(gids[gb] - s * NB, 0, NB - 1)
        for i, src in enumerate((kx, vx)):
            for h in range(HD):
                cand[(i * HD + h) * G + gb] = src[h * NB + mine]

    def gather(t):
        for n, off in enumerate(OFFS + ((0, 0),)):
            code = jnp.maximum(wanted_s[seq_peer(s, off), 0, t], 0)
            stage[n, t, 0] = kx[code]
            stage[n, t, 1] = vx[code]

    def send(t):
        for n, off in enumerate(OFFS):
            pltpu.make_async_remote_copy(
                stage.at[n, t], rand_out.at[s, t], send_r, recv_r,
                device_id=(seq_peer(s, off), hd), device_id_type=MESH,
            ).start()
        pltpu.make_async_copy(stage.at[NS - 1, t], rand_out.at[s, t], recv_r).start()

    gather(0)
    for off in OFFS:
        p = seq_peer(s, off)
        pltpu.make_async_remote_copy(
            cand.at[p], cand_in.at[s], gl_s.at[0], gl_r.at[0], device_id=(p, hd), device_id_type=MESH
        ).start()
    pltpu.make_async_copy(cand.at[s], cand_in.at[s], gl_r.at[0]).start()

    own = []
    for i, (src, dst) in enumerate(((kx, k_out), (vx, v_out))):
        for h in range(HD):
            c = pltpu.make_async_copy(
                src.at[pl.ds(h * NB, NB)], dst.at[h, pl.ds(1, NB)], local.at[2 + i * HD + h]
            )
            c.start()
            own.append(c)

    xs = [(src, dst, dh, h, i) for h in range(HD) for dh in (1, 6, 7, 2, 3, 4, 5)
          for i, (src, dst) in enumerate(((q_in, q_out), (g_in, g_out)))]
    per = -(-len(xs) // CAP)
    for t in range(CAP):
        if t + 1 < CAP:
            gather(t + 1)
        send(t)
        for src, dst, dh, h, i in xs[t * per:(t + 1) * per]:
            x_copy(src, dst, dh, h, recv_qg.at[i]).start()
        if t == 0:
            for h in range(HD):
                x_local(q_in, q_out, h, recv_qg.at[0]).start()
                x_local(g_in, g_out, h, recv_qg.at[1]).start()
        if t == 5:
            pltpu.make_async_copy(cand_in, cand_in, gl_r.at[0]).wait()
            gb = s % G
            owner = lax.div(gids[gb], NB)
            chosen[...] = cand_in[owner]
        if t == 6:
            for off in OFFS:
                pltpu.make_async_remote_copy(
                    chosen, glob_out.at[s], gl_s.at[1], gl_r.at[1],
                    device_id=(seq_peer(s, off), hd), device_id_type=MESH,
                ).start()
            pltpu.make_async_copy(chosen, glob_out.at[s], gl_r.at[1]).start()

    to_out.wait()
    for c in own:
        c.wait()
    tail = pl.ds(0, NS - 1)
    pltpu.make_async_copy(wanted_v.at[tail], wanted_v.at[tail], send_t).wait()
    pltpu.make_async_copy(q_out, q_out, recv_qg.at[0]).wait()
    pltpu.make_async_copy(g_out, g_out, recv_qg.at[1]).wait()
    sent = stage.at[pl.ds(0, NH), pl.ds(0, 14)]
    pltpu.make_async_copy(sent, sent, send_x).wait()
    halo = stage.at[0, pl.ds(0, 8)]
    pltpu.make_async_copy(halo, halo, halo_s).wait()
    pltpu.make_async_copy(halo, halo, halo_r).wait()
    pltpu.make_async_copy(cand.at[tail], cand.at[tail], gl_s.at[0]).wait()
    pltpu.make_async_copy(cand.at[tail], cand.at[tail], gl_s.at[1]).wait()
    pltpu.make_async_copy(glob_out, glob_out, gl_r.at[1]).wait()
    pltpu.make_async_copy(stage.at[tail], stage.at[tail], send_r).wait()
    pltpu.make_async_copy(rand_out, rand_out, recv_r).wait()


def fetch(q, k, v, g, table, gids):
    bf = jnp.bfloat16
    sds = jax.ShapeDtypeStruct
    dma = pltpu.SemaphoreType.DMA
    return pl.pallas_call(
        fetch_kernel,
        name="fetch",
        out_shape=(
            sds((HD * T, W), bf), sds((HD * T, W), bf),
            sds((HD, NB + 2, B, W), bf), sds((HD, NB + 2, B, W), bf),
            sds((NS, CAP, 2, B, W), bf), sds((NS, B, W), bf), sds((NS, 1, 128), jnp.int32),
        ),
        in_specs=[spec(ANY)] * 5 + [spec(pltpu.SMEM)],
        out_specs=(spec(ANY),) * 7,
        scratch_shapes=[
            VM((HD * NB, B, W), bf), VM((HD * NB, B, W), bf), VM((NS, CAP, 2, B, W), bf),
            VM((NS, 1, 128), jnp.int32), pltpu.SMEM((NS, 1, 128), jnp.int32),
            VM((NS, B, W), bf), VM((NS, B, W), bf), VM((B, W), bf),
            dma, dma((2,)), dma((2,)), dma, dma, dma((10,)), dma, dma, dma, dma, dma((2,)), dma((2,)),
        ],
        compiler_params=pltpu.CompilerParams(
            collective_id=0, has_side_effects=True, vmem_limit_bytes=VLIM
        ),
    )(q, k, v, g, table, gids)


def dot(a, b):
    return jnp.dot(a, b, preferred_element_type=jnp.float32)


def dot_nt(a, b):
    return lax.dot_general(a, b, (((1,), (1,)), ((), ())), preferred_element_type=jnp.float32)


def dot_tn(a, b):
    return lax.dot_general(a, b, (((0,), (0,)), ((), ())), preferred_element_type=jnp.float32)


def attend_kernel(
    slots, drops, shard, q_ref, g_ref, k_ref, v_ref, glob_ref, rand_ref,
    att_ref, dq_ref, dkv_ref, gsum_ref, rim_ref, term_ref,
    gk_acc, gv_acc,
):
    h = pl.program_id(0)
    s = shard[0]
    bf = jnp.bfloat16
    dkv_ref[...] = jnp.zeros_like(dkv_ref)
    gk_acc[...] = jnp.zeros_like(gk_acc)
    gv_acc[...] = jnp.zeros_like(gv_acc)
    low = lax.broadcasted_iota(jnp.int32, (1, W), 1) < B
    low2 = lax.broadcasted_iota(jnp.int32, (B, W), 1) < B
    ninf = jnp.float32(-jnp.inf)

    def body(p, carry):
        rows = pl.ds(pl.multiple_of(p * 2 * B, 2 * B), 2 * B)
        ext = pl.ds(pl.multiple_of(p * 2 * B, 2 * B), 4 * B)
        q = q_ref[rows, :]
        g = g_ref[rows, :]
        kwg = jnp.concatenate([k_ref[0, pl.ds(2 * p, 4)].reshape(4 * B, W), glob_ref[0, 0, 0], glob_ref[0, 0, 1]], 0)
        vwg = jnp.concatenate([v_ref[0, pl.ds(2 * p, 4)].reshape(4 * B, W), glob_ref[1, 0, 0], glob_ref[1, 0, 1]], 0)
        at = [[slots[h * NB * R + (2 * p + i) * R + r] for r in range(R)] for i in range(2)]
        kr = [jnp.concatenate([rand_ref[a, 0] for a in at[i]], 0) for i in range(2)]
        vr = [jnp.concatenate([rand_ref[a, 1] for a in at[i]], 0) for i in range(2)]
        keep = [
            [drops[h, 2 * p + i, n].astype(jnp.float32) * (1.0 / KEEP) for n in range(8)]
            for i in range(2)
        ]
        swg = dot_nt(q, kwg)
        dwg = dot_nt(g, vwg)
        halves = []
        for i in range(2):
            hb = slice(i * B, (i + 1) * B)
            sr = dot_nt(q[hb], kr[i])
            dr = dot_nt(g[hb], vr[i])
            c0, c1, c2 = (swg[hb, n * W:(n + 1) * W] for n in range(3))
            absent0 = jnp.logical_and(s == 0, p == 0) if i == 0 else True
            absent3 = jnp.logical_and(s == NS - 1, p == NB // 2 - 1) if i == 1 else True
            c0 = jnp.where(jnp.logical_and(low2, absent0), ninf, c0)
            c1 = jnp.where(jnp.logical_and(jnp.logical_not(low2), absent3), ninf, c1)
            c3, c4 = sr[:, :W], sr[:, W:]
            cols = [c0, c1, c2, c3, c4]
            d = keep[i]
            if i == 0:
                ret = [jnp.where(low, d[0], d[1]), jnp.where(low, d[2], 0.0)]
            else:
                ret = [jnp.where(low, 0.0, d[0]), jnp.where(low, d[1], d[2])]
            ret += [jnp.where(low, d[3], d[4]), jnp.where(low, d[5], d[6])]
            ret += [jnp.full((1, B), d[7], jnp.float32)]
            raw = [dwg[hb, n * W:(n + 1) * W] for n in range(3)] + [dr[:, :W], dr[:, W:]]
            top = jnp.maximum(jnp.maximum(c0, c1), jnp.maximum(c2, c3))
            top = jnp.maximum(
                jnp.max(top, axis=1, keepdims=True), jnp.max(c4, axis=1, keepdims=True)
            )
            e = [jnp.exp2((c - top) * (SCALE * LOG2E)) for c in cols]
            total = jnp.sum(e[0] + e[1] + e[2] + e[3], axis=1, keepdims=True)
            total = total + jnp.sum(e[4], axis=1, keepdims=True)
            inv = 1.0 / total
            pr = [x * inv for x in e]
            dp = [x * y for x, y in zip(raw, ret)]
            pp = [x * y for x, y in zip(pr, dp)]
            delta = jnp.sum(pp[0] + pp[1] + pp[2] + pp[3], axis=1, keepdims=True)
            delta = delta + jnp.sum(pp[4], axis=1, keepdims=True)
            pd = [(x * y).astype(bf) for x, y in zip(pr, ret)]
            ds = [(x * (y - delta)).astype(bf) for x, y in zip(pr, dp)]
            halves.append((pd, ds))
        pd_wg = jnp.concatenate([jnp.concatenate(hv[0][:3], 1) for hv in halves], 0)
        ds_wg = jnp.concatenate([jnp.concatenate(hv[1][:3], 1) for hv in halves], 0)
        pd_r = [jnp.concatenate(hv[0][3:], 1) for hv in halves]
        ds_r = [jnp.concatenate(hv[1][3:], 1) for hv in halves]
        att = dot(pd_wg, vwg) + jnp.concatenate([dot(pd_r[i], vr[i]) for i in range(2)], 0)
        att_ref[rows, :] = att.astype(bf)
        dq = dot(ds_wg, kwg) + jnp.concatenate([dot(ds_r[i], kr[i]) for i in range(2)], 0)
        dq_ref[rows, :] = (dq * SCALE).astype(bf)
        dk = dot_tn(ds_wg, q) * SCALE
        dv = dot_tn(pd_wg, g)
        dkv_ref[0, 0, ext, :] += dk[:4 * B]
        dkv_ref[1, 0, ext, :] += dv[:4 * B]
        gk_acc[...] += dk[4 * B:]
        gv_acc[...] += dv[4 * B:]
        for i in range(2):
            hb = slice(i * B, (i + 1) * B)
            dkr = (dot_tn(ds_r[i], q[hb]) * SCALE).astype(bf)
            dvr = dot_tn(pd_r[i], g[hb]).astype(bf)
            for r in range(R):
                term_ref[at[i][r], 0] = dkr[r * B:(r + 1) * B]
                term_ref[at[i][r], 1] = dvr[r * B:(r + 1) * B]
        return carry

    lax.fori_loop(0, NB // 2, body, 0)
    for i, gacc in enumerate((gk_acc, gv_acc)):
        for gb in range(G):
            gsum_ref[i, 0, gb] = gacc[gb * B:(gb + 1) * B].astype(bf)
        rim_ref[0, i, 0] = dkv_ref[i, 0, :B].astype(bf)
        rim_ref[1, i, 0] = dkv_ref[i, 0, B + T:].astype(bf)


def attend(slots, drops, shard, q, g, k, v, glob, rand):
    bf = jnp.bfloat16
    f32 = jnp.float32
    sds = jax.ShapeDtypeStruct
    sm = spec(pltpu.SMEM)
    E = T + 2 * B
    return pl.pallas_call(
        attend_kernel,
        name="attend",
        grid=(HD,),
        out_shape=(
            sds((T, HD * W), bf), sds((T, HD * W), bf),
            sds((2, HD, E, W), f32),
            sds((2, HD, G, B, W), bf), sds((2, 2, HD, B, W), bf),
            sds((NS * CAP, 2, B, W), bf),
        ),
        in_specs=[
            sm, sm, sm,
            pl.BlockSpec((T, W), lambda h: (h, 0)),
            pl.BlockSpec((T, W), lambda h: (h, 0)),
            pl.BlockSpec((1, NB + 2, B, W), lambda h: (h, 0, 0, 0)),
            pl.BlockSpec((1, NB + 2, B, W), lambda h: (h, 0, 0, 0)),
            pl.BlockSpec((2, 1, G, B, W), lambda h: (0, h, 0, 0, 0)),
            pl.BlockSpec((NS * CAP, 2, B, W), lambda h: (0, 0, 0, 0), pipeline_mode=pl.Buffered(1)),
        ],
        out_specs=(
            pl.BlockSpec((T, W), lambda h: (0, h)),
            pl.BlockSpec((T, W), lambda h: (0, h)),
            pl.BlockSpec((2, 1, E, W), lambda h: (0, h, 0, 0)),
            pl.BlockSpec((2, 1, G, B, W), lambda h: (0, h, 0, 0, 0)),
            pl.BlockSpec((2, 2, 1, B, W), lambda h: (0, 0, h, 0, 0)),
            pl.BlockSpec((NS * CAP, 2, B, W), lambda h: (0, 0, 0, 0)),
        ),
        scratch_shapes=[VM((G * B, W), f32), VM((G * B, W), f32)],
        compiler_params=pltpu.CompilerParams(vmem_limit_bytes=VLIM),
    )(slots, drops, shard, q, g, k, v, glob, rand)


def give_back_kernel(
    term, rim, gsum, ret, rim_out, gtot, part, total, send_r, recv_r, rim_s, rim_r, gl_s, gl_r
):
    s = lax.axis_index("seq")
    hd = lax.axis_index("head")
    barrier = pltpu.get_barrier_semaphore()
    for off in OFFS:
        pl.semaphore_signal(barrier, inc=1, device_id=(seq_peer(s, off), hd), device_id_type=MESH)
    pl.semaphore_wait(barrier, NS - 1)

    for off in OFFS:
        p = seq_peer(s, off)
        pltpu.make_async_remote_copy(
            gsum.at[p], part.at[s], gl_s.at[0], gl_r.at[0], device_id=(p, hd), device_id_type=MESH
        ).start()
    pltpu.make_async_copy(gsum.at[s], part.at[s], gl_r.at[0]).start()
    prv = (s + NS - 1) % NS
    nxt = (s + 1) % NS
    pltpu.make_async_remote_copy(
        rim.at[0], rim_out.at[1], rim_s, rim_r, device_id=(prv, hd), device_id_type=MESH
    ).start()
    pltpu.make_async_remote_copy(
        rim.at[1], rim_out.at[0], rim_s, rim_r, device_id=(nxt, hd), device_id_type=MESH
    ).start()

    def send(t):
        for off in OFFS:
            p = seq_peer(s, off)
            pltpu.make_async_remote_copy(
                term.at[p, t], ret.at[s, t], send_r, recv_r, device_id=(p, hd), device_id_type=MESH
            ).start()
        pltpu.make_async_copy(term.at[s, t], ret.at[s, t], recv_r).start()

    for t in range(CAP):
        send(t)
        if t == 2:
            pltpu.make_async_copy(part, part, gl_r.at[0]).wait()
            acc = part[0].astype(jnp.float32)
            for i in range(1, NS):
                acc = acc + part[i].astype(jnp.float32)
            total[...] = acc.astype(jnp.bfloat16)
        if t == 3:
            for off in OFFS:
                pltpu.make_async_remote_copy(
                    total, gtot.at[s], gl_s.at[1], gl_r.at[1],
                    device_id=(seq_peer(s, off), hd), device_id_type=MESH,
                ).start()
            pltpu.make_async_copy(total, gtot.at[s], gl_r.at[1]).start()

    tail = pl.ds(0, NS - 1)
    pltpu.make_async_copy(rim, rim, rim_s).wait()
    pltpu.make_async_copy(rim_out, rim_out, rim_r).wait()
    pltpu.make_async_copy(part.at[tail], part.at[tail], gl_s.at[0]).wait()
    pltpu.make_async_copy(part.at[tail], part.at[tail], gl_s.at[1]).wait()
    pltpu.make_async_copy(gtot, gtot, gl_r.at[1]).wait()
    pltpu.make_async_copy(term.at[tail], term.at[tail], send_r).wait()
    pltpu.make_async_copy(ret, ret, recv_r).wait()


def give_back(term, rim, gsum):
    bf = jnp.bfloat16
    sds = jax.ShapeDtypeStruct
    dma = pltpu.SemaphoreType.DMA
    return pl.pallas_call(
        give_back_kernel,
        name="give_back",
        out_shape=(
            sds((NS, CAP, 2, B, W), bf), sds((2, 2, HD, B, W), bf), sds((NS, B, W), bf),
        ),
        in_specs=[spec(ANY)] * 3,
        out_specs=(spec(ANY),) * 3,
        scratch_shapes=[
            VM((NS, B, W), bf), VM((B, W), bf),
            dma, dma, dma, dma, dma((2,)), dma((2,)),
        ],
        compiler_params=pltpu.CompilerParams(
            collective_id=1, has_side_effects=True, vmem_limit_bytes=VLIM
        ),
    )(term, rim, gsum)


def gather_up_kernel(wanted, gids, shard, dext, rim, gtot, ret, dk_ref, dv_ref, acc):
    s = shard[0]
    i = pl.program_id(0)

    def go(dext):
        for h in range(HD):
            acc[h * T:(h + 1) * T] = dext[0, h, B:B + T]

            @pl.when(s > 0)
            def _():
                acc[h * T:h * T + B] += rim[0, 0, h].astype(jnp.float32)

            @pl.when(s < NS - 1)
            def _():
                acc[h * T + T - B:h * T + T] += rim[1, 0, h].astype(jnp.float32)

            for gb in range(G):
                local = gids[gb] - s * NB

                @pl.when(jnp.logical_and(local >= 0, local < NB))
                def _():
                    at = pl.ds(pl.multiple_of(h * T + local * B, B), B)
                    acc[at, :] += gtot[0, h, gb].astype(jnp.float32)

    go(dext)

    def add(n, c):
        lister = n // CAP
        code = wanted[lister, 0, n % CAP]

        @pl.when(code >= 0)
        def _():
            at = pl.ds(pl.multiple_of(code * B, B), B)
            acc[at, :] += ret[n, 0].astype(jnp.float32)

        return c

    lax.fori_loop(0, NS * CAP, add, 0)
    for n, out in enumerate((dk_ref, dv_ref)):

        @pl.when(i == n)
        def _():
            for h in range(HD):
                out[:, h * W:(h + 1) * W] = acc[h * T:(h + 1) * T].astype(jnp.bfloat16)


def gather_up(wanted, gids, shard, dext, rim, gtot, ret):
    sds = jax.ShapeDtypeStruct
    sm = spec(pltpu.SMEM)
    E = T + 2 * B
    return pl.pallas_call(
        gather_up_kernel,
        name="gather_up",
        grid=(2,),
        out_shape=(sds((T, HD * W), jnp.bfloat16),) * 2,
        in_specs=[
            sm, sm, sm,
            pl.BlockSpec((1, HD, E, W), lambda i: (i, 0, 0, 0)),
            pl.BlockSpec((2, 1, HD, B, W), lambda i: (0, i, 0, 0, 0)),
            pl.BlockSpec((1, HD, G, B, W), lambda i: (i, 0, 0, 0, 0)),
            pl.BlockSpec((NS * CAP, 1, B, W), lambda i: (0, i, 0, 0)),
        ],
        out_specs=(pl.BlockSpec((T, HD * W), lambda i: (0, 0)),) * 2,
        scratch_shapes=[VM((HD * T, W), jnp.float32)],
        compiler_params=pltpu.CompilerParams(vmem_limit_bytes=VLIM),
    )(wanted, gids, shard, dext, rim, gtot, ret)


def per_device(queries, keys, values, grad_out, rand_blocks, global_ids, drop_mask):
    shard = lax.axis_index("seq").astype(jnp.int32).reshape(1)
    table, slots = request_table(rand_blocks.reshape(-1))
    q, g, k, v, rand, glob, wanted = fetch(queries, keys, values, grad_out, table, global_ids)
    att, dq, dkv, gsum, rim, term = attend(
        slots, drop_mask, shard, q, g, k, v,
        glob.reshape(2, HD, G, B, W), rand.reshape(NS * CAP, 2, B, W),
    )
    ret, rim_in, gtot = give_back(term.reshape(NS, CAP, 2, B, W), rim, gsum.reshape(NS, B, W))
    dk, dv = gather_up(
        wanted, global_ids, shard, dkv, rim_in,
        gtot.reshape(2, HD, G, B, W), ret.reshape(NS * CAP, 2, B, W),
    )
    return att, dq, dk, dv


def solution(mesh):
    rows = P(("seq", "head"), None)
    out = P("seq", "head")
    return jax.shard_map(
        per_device,
        mesh=mesh,
        in_specs=(rows, rows, rows, rows, P("head", "seq", None), P(), P("head", "seq", None)),
        out_specs=(out, out, out, out),
        check_vma=False,
    )
```

```python
import functools
import math

import jax
import jax.numpy as jnp
from jax import lax
from jax.experimental import pallas as pl
from jax.experimental.pallas import tpu as pltpu
from jax.sharding import PartitionSpec as P

W = 128
B = 64
R = 3
G = 2
NS = 16
NH = 8
HD = 4
NB = 16
EB = NB + 2
CAP = 15
REQ = HD * NB * R
T = NB * B
KEEP = 0.9
SCALE = W**-0.5
LOG2E = math.log2(math.e)
MESH = pl.DeviceIdType.MESH
VM = pltpu.VMEM
ANY = pl.ANY
VLIM = 62 * 1024 * 1024

OFFS = (
    (0, 1), (1, 0), (0, 3), (3, 0), (0, 2), (2, 0), (1, 1), (3, 3),
    (1, 3), (3, 1), (1, 2), (2, 1), (3, 2), (2, 3), (2, 2),
)


def seq_peer(s, off):
    return ((s // 4 + off[0]) % 4) * 4 + (s % 4 + off[1]) % 4


def spec(space):
    return pl.BlockSpec(memory_space=space)


def table_kernel(ids_ref, table_ref, inverse_ref, slot_ref, count):
    def clear(i, c):
        for o in range(NS):
            table_ref[o, 0, i] = -1
            inverse_ref[o, 0, i] = 0
        return c

    lax.fori_loop(0, CAP, clear, 0)
    for o in range(NS):
        count[o] = 0

    for r in range(R):

        def one(i, c):
            h = i // NB
            block = ids_ref[r, h, i % NB]
            owner = block // NB
            rank = count[owner]
            count[owner] = rank + 1
            table_ref[owner, 0, rank] = h * EB + 1 + block % NB
            inverse_ref[owner, 0, rank] = r * HD * NB + i
            slot_ref[r * HD * NB + i] = owner * CAP + rank
            return c

        lax.fori_loop(0, HD * NB, one, 0)


def request_table(ids):
    sm = spec(pltpu.SMEM)
    tab = jax.ShapeDtypeStruct((NS, 1, 128), jnp.int32)
    return pl.pallas_call(
        table_kernel,
        name="request_table",
        out_shape=(tab, tab, jax.ShapeDtypeStruct((REQ,), jnp.int32)),
        in_specs=[sm],
        out_specs=(sm, sm, sm),
        scratch_shapes=[pltpu.SMEM((NS,), jnp.int32)],
    )(ids)


def dot(a, b):
    return jnp.dot(a, b, preferred_element_type=jnp.float32)


def dot_nt(a, b):
    return lax.dot_general(a, b, (((1,), (1,)), ((), ())), preferred_element_type=jnp.float32)


def dot_tn(a, b):
    return lax.dot_general(a, b, (((0,), (0,)), ((), ())), preferred_element_type=jnp.float32)


def keep_rows(drops, h, j, half, low):
    d = [drops[h, n, j].astype(jnp.float32) * (1.0 / KEEP) for n in range(8)]
    if half == 0:
        ret = [jnp.where(low, d[0], d[1]), jnp.where(low, d[2], 0.0)]
    else:
        ret = [jnp.where(low, 0.0, d[0]), jnp.where(low, d[1], d[2])]
    ret += [jnp.where(low, d[3], d[4]), jnp.where(low, d[5], d[6])]
    return ret + [jnp.full((1, B), d[7], jnp.float32)]


COLS = ((0, 128), (128, 256), (256, 384), (384, 512), (512, 576))


def wide_sum(cols):
    return jnp.sum(cols[0] + cols[1] + cols[2] + cols[3], axis=1, keepdims=True) + jnp.sum(
        cols[4], axis=1, keepdims=True
    )


def main_kernel(
    q_in, k_in, v_in, g_in, table, inverse, slots, drops, gids,
    att_out, dq_out, acc_out, ret_out, rim_out, gtot_out, wanted_out,
    kx, vx, qx, gx, kh, vh, sk, sv, rk, rv, probs, tk, tv, acck, accv, gacck, gaccv, att_v, dq_v,
    wanted_v, wanted_s, cand, cand_k, cand_v, chosen, glob, gsum, gpart, gdone, rim,
    send_x, recv_x, send_t, recv_t, local, send_r, recv_r, halo_s, halo_r, gl_s, gl_r, rim_s, rim_r,
):
    f32, bf = jnp.float32, jnp.bfloat16
    s = lax.axis_index("seq")
    hd = lax.axis_index("head")
    nxt = (s + 1) % NS
    prv = (s + NS - 1) % NS
    tail = pl.ds(0, NS - 1)

    def remote(src, dst, ssem, rsem, peer):
        pltpu.make_async_remote_copy(
            src, dst, ssem, rsem, device_id=(peer, hd), device_id_type=MESH
        ).start()

    def near(src, dst, sem):
        pltpu.make_async_copy(src, dst, sem).start()

    def drain(view, sem):
        pltpu.make_async_copy(view, view, sem).wait()

    def everyone(src, dst, ssem, rsem):
        for off in OFFS:
            p = seq_peer(s, off)
            remote(src(p), dst, ssem, rsem, p)
        near(src(s), dst, rsem)

    barrier = pltpu.get_barrier_semaphore()
    for off in OFFS:
        pl.semaphore_signal(barrier, inc=1, device_id=(seq_peer(s, off), hd), device_id_type=MESH)
    for dh in range(1, NH):
        pl.semaphore_signal(barrier, inc=1, device_id=(s, (hd + dh) % NH), device_id_type=MESH)
    pl.semaphore_wait(barrier, NS - 1 + NH - 1)

    def tiles(n):
        src, dst = ((k_in, kx), (v_in, vx))[n]
        for h in range(HD):
            for i in range(2):
                yield src, pl.ds(i * B, B), h, dst.at[h * EB + 1 + hd * 2 + i], n

    def rows(n):
        src, dst = ((q_in, qx), (g_in, gx))[n]
        for h in range(HD):
            at = pl.ds(pl.multiple_of(h * T + hd * 128, 128), 128)
            yield src, slice(None), h, dst.at[at, :], 2 + n

    def pieces(group):
        for src, at, h, dst, n in group:
            for dh in (1, 6, 7, 2, 3, 4, 5, 0):
                yield src, at, h, dst, n, dh

    def over_x(piece):
        src, at, h, dst, n, dh = piece
        p = (hd + dh) % NH
        a = src.at[at, pl.ds(pl.multiple_of((p * HD + h) * W, W), W)]
        if dh == 0:
            near(a, dst, recv_x.at[n])
        else:
            pltpu.make_async_remote_copy(
                a, dst, send_x, recv_x.at[n], device_id=(s, p), device_id_type=MESH
            ).start()

    for piece in pieces(tiles(0)):
        over_x(piece)
    everyone(lambda p: table.at[p], wanted_v.at[s], send_t, recv_t)
    later = list(pieces(tiles(1))) + list(pieces(rows(0))) + list(pieces(rows(1)))
    cuts = [0, 16, 28, 40, 52, 64] + [64 + 7 * n for n in range(1, 10)] + [len(later)]

    drain(wanted_v, recv_t)
    to_scalar = pltpu.make_async_copy(wanted_v, wanted_s, local.at[0])
    to_scalar.start()
    near(wanted_v, wanted_out, local.at[1])
    to_scalar.wait()

    def spread_blocks(n, x, stage, landing, extra):
        halo = (kh, vh)[n]
        cand_in = (cand_k, cand_v)[n]
        for h in range(HD):
            remote(x.at[h * EB + NB], halo.at[0, h], halo_s.at[n], halo_r.at[n], nxt)
            remote(x.at[h * EB + 1], halo.at[1, h], halo_s.at[n], halo_r.at[n], prv)
        for gb in range(G):
            mine = jnp.clip(gids[gb] - s * NB, 0, NB - 1)
            for h in range(HD):
                tile = x[h * EB + 1 + mine]
                for half in range(2):
                    cand[n, h * 4 + gb * 2 + half] = tile[half * 32:half * 32 + 32]

        def gather(t):
            for m, off in enumerate(OFFS + ((0, 0),)):
                code = jnp.maximum(wanted_s[seq_peer(s, off), 0, t], 0)
                stage[m, t] = x[code]

        def send(t):
            for m, off in enumerate(OFFS):
                remote(
                    stage.at[m, t], landing.at[s * CAP + t], send_r.at[n], recv_r.at[n],
                    seq_peer(s, off),
                )
            near(stage.at[NS - 1, t], landing.at[s * CAP + t], recv_r.at[n])

        gather(0)
        everyone(lambda p: cand.at[n, p], cand_in.at[s], gl_s.at[2 * n], gl_r.at[2 * n])
        for t in range(CAP):
            if t + 1 < CAP:
                gather(t + 1)
            send(t)
            for piece in later[cuts[t]:cuts[t + 1]] if extra else ():
                over_x(piece)
            if t == 5:
                drain(cand_in, gl_r.at[2 * n])
                owner = lax.div(gids[lax.rem(lax.div(s, 2), 2)], NB)
                chosen[n] = cand_in[owner]
            if t == 6:
                everyone(
                    lambda p: chosen.at[n], glob.at[n, s], gl_s.at[2 * n + 1], gl_r.at[2 * n + 1]
                )

    def await_blocks(n, x, landing):
        halo = (kh, vh)[n]
        drain(halo, halo_r.at[n])
        for h in range(HD):
            x[h * EB] = halo[0, h]
            x[h * EB + NB + 1] = halo[1, h]
        drain(glob.at[n], gl_r.at[2 * n + 1])
        drain(landing, recv_r.at[n])

    drain(kx.at[pl.ds(0, HD * NB)], recv_x.at[0])
    spread_blocks(0, kx, sk, rk, True)
    drain(vx.at[pl.ds(0, HD * NB)], recv_x.at[1])
    spread_blocks(1, vx, sv, rv, False)

    accv[...] = jnp.zeros_like(accv)
    acck[...] = jnp.zeros_like(acck)
    gaccv[...] = jnp.zeros_like(gaccv)
    gacck[...] = jnp.zeros_like(gacck)
    drain(qx, recv_x.at[2])
    drain(gx, recv_x.at[3])
    await_blocks(0, kx, rk)

    low = lax.broadcasted_iota(jnp.int32, (1, W), 1) < B
    low2 = lax.broadcasted_iota(jnp.int32, (B, W), 1) < B
    ninf = f32(-jnp.inf)

    def place(i):
        h = lax.div(i, NB // 2)
        p = lax.rem(i, NB // 2)
        at = pl.ds(pl.multiple_of(i * 2 * B, 2 * B), 2 * B)
        ext = pl.ds(pl.multiple_of(p * 2 * B, 2 * B), 4 * B)
        return h, p, at, ext

    def listed(n, x, landing, h, p):
        window = x[pl.ds(h * EB + 2 * p, 4)].reshape(4 * B, W)
        wide = glob[n, pl.ds(h * 4, 4)].reshape(2 * B, W)
        rand = []
        for half in range(2):
            own = [landing[slots[r * HD * NB + h * NB + 2 * p + half]] for r in range(R)]
            rand.append(jnp.concatenate(own, 0))
        return jnp.concatenate([window, wide], 0), rand

    def store_terms(term, h, p, half, tiles):
        for r in range(R):
            term[r * HD * NB + h * NB + 2 * p + half] = tiles[r * B:(r + 1) * B]

    def phase1(i, c):
        h, p, at, ext = place(i)
        q = qx[at, :]
        g = gx[at, :]
        kwg, kr = listed(0, kx, rk, h, p)
        swg = dot_nt(q, kwg)
        pds = []
        for half in range(2):
            hb = slice(half * B, (half + 1) * B)
            sr = dot_nt(q[hb], kr[half])
            c0, c1, c2 = (swg[hb, n * W:(n + 1) * W] for n in range(3))
            absent0 = jnp.logical_and(s == 0, p == 0) if half == 0 else True
            absent3 = jnp.logical_and(s == NS - 1, p == NB // 2 - 1) if half == 1 else True
            c0 = jnp.where(jnp.logical_and(low2, absent0), ninf, c0)
            c1 = jnp.where(jnp.logical_and(jnp.logical_not(low2), absent3), ninf, c1)
            cols = [c0, c1, c2, sr[:, :W], sr[:, W:]]
            top = jnp.maximum(jnp.maximum(c0, c1), jnp.maximum(c2, cols[3]))
            top = jnp.maximum(
                jnp.max(top, axis=1, keepdims=True), jnp.max(cols[4], axis=1, keepdims=True)
            )
            e = [jnp.exp2((x - top) * (SCALE * LOG2E)) for x in cols]
            inv = 1.0 / wide_sum(e)
            pr = [x * inv for x in e]
            for (a, b), x in zip(COLS, pr):
                probs[i, hb, a:b] = x
            ret = keep_rows(drops, h, 2 * p + half, half, low)
            pds.append([(x * y).astype(bf) for x, y in zip(pr, ret)])
        pd_wg = jnp.concatenate([jnp.concatenate(x[:3], 1) for x in pds], 0)
        dv = dot_tn(pd_wg, g)
        accv[h, ext, :] += dv[:4 * B]
        gaccv[h] += dv[4 * B:]
        for half in range(2):
            dvr = dot_tn(jnp.concatenate(pds[half][3:], 1), g[half * B:(half + 1) * B])
            store_terms(tv, h, p, half, dvr.astype(bf))
        return c

    def phase2(i, c):
        h, p, at, ext = place(i)
        q = qx[at, :]
        g = gx[at, :]
        kwg, kr = listed(0, kx, rk, h, p)
        vwg, vr = listed(1, vx, rv, h, p)
        dwg = dot_nt(g, vwg)
        halves = []
        for half in range(2):
            hb = slice(half * B, (half + 1) * B)
            dr = dot_nt(g[hb], vr[half])
            raw = [dwg[hb, n * W:(n + 1) * W] for n in range(3)] + [dr[:, :W], dr[:, W:]]
            pr = [probs[i, hb, a:b] for a, b in COLS]
            ret = keep_rows(drops, h, 2 * p + half, half, low)
            dp = [x * y for x, y in zip(raw, ret)]
            delta = wide_sum([x * y for x, y in zip(pr, dp)])
            pd = [(x * y).astype(bf) for x, y in zip(pr, ret)]
            ds = [(x * (y - delta)).astype(bf) for x, y in zip(pr, dp)]
            halves.append((pd, ds))
        pd_wg = jnp.concatenate([jnp.concatenate(x[0][:3], 1) for x in halves], 0)
        ds_wg = jnp.concatenate([jnp.concatenate(x[1][:3], 1) for x in halves], 0)
        pd_r = [jnp.concatenate(x[0][3:], 1) for x in halves]
        ds_r = [jnp.concatenate(x[1][3:], 1) for x in halves]
        att = dot(pd_wg, vwg) + jnp.concatenate([dot(a, b) for a, b in zip(pd_r, vr)], 0)
        att_v[at, :] = att.astype(bf)
        dq = dot(ds_wg, kwg) + jnp.concatenate([dot(a, b) for a, b in zip(ds_r, kr)], 0)
        dq_v[at, :] = (dq * SCALE).astype(bf)
        dk = dot_tn(ds_wg, q) * SCALE
        acck[h, ext, :] += dk[:4 * B]
        gacck[h] += dk[4 * B:]
        for half in range(2):
            dkr = dot_tn(ds_r[half], q[half * B:(half + 1) * B]) * SCALE
            store_terms(tk, h, p, half, dkr.astype(bf))
        return c

    def give_back(n, m, acc, gacc, term, stage):
        for h in range(HD):
            rim[n, 0, h] = acc[h, :B].astype(bf)
            rim[n, 1, h] = acc[h, B + T:].astype(bf)
            for c in range(4):
                gsum[n, h * 4 + c] = gacc[h, c * 32:(c + 1) * 32].astype(bf)
        near(acc, acc_out.at[n], local.at[2 + n])

        def gather(t):
            for j, off in enumerate(OFFS + ((0, 0),)):
                stage[j, t] = term[inverse[seq_peer(s, off), 0, t]]

        def send(t):
            for j, off in enumerate(OFFS):
                remote(
                    stage.at[j, t], ret_out.at[n, s, t], send_r.at[m], recv_r.at[m],
                    seq_peer(s, off),
                )
            near(stage.at[NS - 1, t], ret_out.at[n, s, t], recv_r.at[m])

        gather(0)
        everyone(lambda p: gsum.at[n, p], gpart.at[n, s], gl_s.at[2 * m], gl_r.at[2 * m])
        remote(rim.at[n, 0], rim_out.at[n, 1], rim_s.at[n], rim_r.at[n], prv)
        remote(rim.at[n, 1], rim_out.at[n, 0], rim_s.at[n], rim_r.at[n], nxt)
        for t in range(CAP):
            if t + 1 < CAP:
                gather(t + 1)
            send(t)
            if t == 5:
                drain(gpart.at[n], gl_r.at[2 * m])
                total = gpart[n, 0].astype(f32)
                for i in range(1, NS):
                    total = total + gpart[n, i].astype(f32)
                gdone[n] = total.astype(bf)
            if t == 6:
                everyone(
                    lambda p: gdone.at[n], gtot_out.at[n, s], gl_s.at[2 * m + 1],
                    gl_r.at[2 * m + 1],
                )

    lax.fori_loop(0, HD * NB // 2, phase1, 0)
    drain(sk.at[tail], send_r.at[0])
    give_back(1, 2, accv, gaccv, tv, sk)
    await_blocks(1, vx, rv)
    lax.fori_loop(0, HD * NB // 2, phase2, 0)
    drain(sv.at[tail], send_r.at[1])
    give_back(0, 3, acck, gacck, tk, sv)
    for h in range(HD):
        near(att_v.at[pl.ds(h * T, T), :], att_out.at[:, pl.ds(h * W, W)], local.at[4])
        near(dq_v.at[pl.ds(h * T, T), :], dq_out.at[:, pl.ds(h * W, W)], local.at[5])

    drain(wanted_v, local.at[1])
    drain(wanted_v.at[tail], send_t)
    drain(rk.at[pl.ds(0, 7 * 4 * 8)], send_x)
    for n in range(2):
        drain(kh, halo_s.at[n])
        drain(rim.at[n], rim_s.at[n])
        drain(rim_out.at[n], rim_r.at[n])
        drain((acck, accv)[n], local.at[2 + n])
    for m in range(8):
        drain(glob.at[0, tail], gl_s.at[m])
    drain(gtot_out.at[1], gl_r.at[5])
    drain(gtot_out.at[0], gl_r.at[7])
    drain(att_v, local.at[4])
    drain(dq_v, local.at[5])
    drain(sk.at[tail], send_r.at[2])
    drain(ret_out.at[1], recv_r.at[2])
    drain(sv.at[tail], send_r.at[3])
    drain(ret_out.at[0], recv_r.at[3])


def main_call(q, k, v, g, table, inverse, slots, drops, gids):
    bf, f32 = jnp.bfloat16, jnp.float32
    sds = jax.ShapeDtypeStruct
    dma = pltpu.SemaphoreType.DMA
    sm = spec(pltpu.SMEM)
    tile = (B, W)
    chunk = (NS, 32, W)
    return pl.pallas_call(
        main_kernel,
        name="exchange_attend",
        out_shape=(
            sds((T, HD * W), bf), sds((T, HD * W), bf), sds((2, HD, EB * B, W), f32),
            sds((2, NS, CAP) + tile, bf), sds((2, 2, HD) + tile, bf), sds((2,) + chunk, bf),
            sds((NS, 1, 128), jnp.int32),
        ),
        in_specs=[spec(ANY)] * 5 + [sm] * 4,
        out_specs=(spec(ANY),) * 7,
        scratch_shapes=[
            VM((HD * EB,) + tile, bf), VM((HD * EB,) + tile, bf),
            VM((HD * T, W), bf), VM((HD * T, W), bf),
            VM((2, HD) + tile, bf), VM((2, HD) + tile, bf),
            VM((NS, CAP) + tile, bf), VM((NS, CAP) + tile, bf),
            VM((NS * CAP,) + tile, bf), VM((NS * CAP,) + tile, bf),
            VM((HD * NB // 2, 2 * B, 640), f32),
            VM((REQ,) + tile, bf), VM((REQ,) + tile, bf),
            VM((HD, EB * B, W), f32), VM((HD, EB * B, W), f32),
            VM((HD, 2 * B, W), f32), VM((HD, 2 * B, W), f32),
            VM((HD * T, W), bf), VM((HD * T, W), bf),
            VM((NS, 1, 128), jnp.int32), pltpu.SMEM((NS, 1, 128), jnp.int32),
            VM((2,) + chunk, bf), VM(chunk, bf), VM(chunk, bf), VM((2, 32, W), bf), VM((2,) + chunk, bf),
            VM((2,) + chunk, bf), VM((2,) + chunk, bf), VM((2, 32, W), bf),
            VM((2, 2, HD) + tile, bf),
            dma, dma((4,)), dma, dma, dma((6,)), dma((4,)), dma((4,)),
            dma((2,)), dma((2,)), dma((8,)), dma((8,)), dma((2,)), dma((2,)),
        ],
        compiler_params=pltpu.CompilerParams(
            collective_id=0, has_side_effects=True, vmem_limit_bytes=VLIM
        ),
    )(q, k, v, g, table, inverse, slots, drops, gids)


def gather_up_kernel(
    wanted, gids, shard, acc_in, rim, gtot, ret, att_in, dq_in, dk_ref, dv_ref, att_ref, dq_ref, acc
):
    s = shard[0]
    i = pl.program_id(0)
    f32 = jnp.float32
    att_ref[...] = att_in[...]
    dq_ref[...] = dq_in[...]
    for h in range(HD):
        for b in range(NB):
            at = slice((b + 1) * B, (b + 2) * B)
            acc[h * EB + 1 + b] = acc_in[0, h, at]

        @pl.when(s > 0)
        def _():
            acc[h * EB + 1] += rim[0, 0, h].astype(f32)

        @pl.when(s < NS - 1)
        def _():
            acc[h * EB + NB] += rim[0, 1, h].astype(f32)

        for gb in range(G):
            mine = gids[gb] - s * NB

            @pl.when(jnp.logical_and(mine >= 0, mine < NB))
            def _():
                acc[h * EB + 1 + mine] += gtot[0, pl.ds(h * 4 + gb * 2, 2)].reshape(B, W).astype(f32)

    def add(lister, c):
        for t in range(CAP):
            code = wanted[lister, 0, t]
            at = jnp.where(code < 0, HD * EB, code)
            acc[at] += ret[0, lister, t].astype(f32)
        return c

    lax.fori_loop(0, NS, add, 0)
    for n, out in enumerate((dk_ref, dv_ref)):

        @pl.when(i == n)
        def _():
            for h in range(HD):
                for b in range(NB):
                    out[b * B:(b + 1) * B, h * W:(h + 1) * W] = acc[h * EB + 1 + b].astype(jnp.bfloat16)


def gather_up(wanted, gids, shard, acc, rim, gtot, ret, att, dq):
    sds = jax.ShapeDtypeStruct
    sm = spec(pltpu.SMEM)
    whole = pl.BlockSpec((T, HD * W), lambda i: (0, 0))
    part = pl.BlockSpec((T // 2, HD * W), lambda i: (i, 0))
    return pl.pallas_call(
        gather_up_kernel,
        name="gather_up",
        grid=(2,),
        out_shape=(sds((T, HD * W), jnp.bfloat16),) * 4,
        in_specs=[
            sm, sm, sm,
            pl.BlockSpec((1, HD, EB * B, W), lambda i: (i, 0, 0, 0)),
            pl.BlockSpec((1, 2, HD, B, W), lambda i: (i, 0, 0, 0, 0)),
            pl.BlockSpec((1, NS, 32, W), lambda i: (i, 0, 0, 0)),
            pl.BlockSpec((1, NS, CAP, B, W), lambda i: (i, 0, 0, 0, 0)),
            part, part,
        ],
        out_specs=(whole, whole, part, part),
        scratch_shapes=[VM((HD * EB + 1, B, W), jnp.float32)],
        compiler_params=pltpu.CompilerParams(vmem_limit_bytes=VLIM),
    )(wanted, gids, shard, acc, rim, gtot, ret, att, dq)


def per_device(queries, keys, values, grad_out, rand_blocks, global_ids, drop_mask):
    shard = lax.axis_index("seq").astype(jnp.int32).reshape(1)
    table, inverse, slots = request_table(rand_blocks.transpose(2, 0, 1))
    att, dq, acc, ret, rim, gtot, wanted = main_call(
        queries, keys, values, grad_out, table, inverse, slots,
        drop_mask.transpose(0, 2, 1), global_ids,
    )
    dk, dv, att, dq = gather_up(wanted, global_ids, shard, acc, rim, gtot, ret, att, dq)
    return att, dq, dk, dv


def solution(mesh):
    rows = P(("seq", "head"), None)
    out = P("seq", "head")
    return jax.shard_map(
        per_device,
        mesh=mesh,
        in_specs=(rows, rows, rows, rows, P("head", "seq", None), P(), P("head", "seq", None)),
        out_specs=(out, out, out, out),
        check_vma=False,
    )
```

```python
import functools
import math

import jax
import jax.numpy as jnp
from jax import lax
from jax.experimental import pallas as pl
from jax.experimental.pallas import tpu as pltpu
from jax.sharding import PartitionSpec as P

W = 128
B = 64
R = 3
G = 2
NS = 16
NH = 8
HD = 4
NB = 16
EB = NB + 2
CAP = 12
EXTRA = 3
REQ = HD * NB * R
T = NB * B
KEEP = 0.9
SCALE = W**-0.5
LOG2E = math.log2(math.e)
MESH = pl.DeviceIdType.MESH
VM = pltpu.VMEM
ANY = pl.ANY
VLIM = 62 * 1024 * 1024

OFFS = (
    (0, 1), (1, 0), (0, 3), (3, 0), (0, 2), (2, 0), (1, 1), (3, 3),
    (1, 3), (3, 1), (1, 2), (2, 1), (3, 2), (2, 3), (2, 2),
)


def seq_peer(s, off):
    return ((s // 4 + off[0]) % 4) * 4 + (s % 4 + off[1]) % 4


def spec(space):
    return pl.BlockSpec(memory_space=space)


def table_kernel(ids_ref, table_ref, inverse_ref, slot_ref, extra_ref):
    def clear(i, c):
        for o in range(NS):
            table_ref[o, 0, i] = -1
            inverse_ref[o, 0, i] = 0
        return c

    lax.fori_loop(0, CAP + EXTRA, clear, 0)
    carry = (jnp.int32(0), jnp.int32(0), jnp.int32(0))
    for r in range(R):

        def one(i, carry):
            low, high, hot = carry
            h = lax.shift_right_logical(i, 4)
            block = ids_ref[r, h, i & (NB - 1)]
            owner = lax.shift_right_logical(block, 4)
            shift = (owner & 7) * 4
            upper = owner >= NS // 2
            rank = lax.shift_right_logical(jnp.where(upper, high, low), shift) & 15
            step = lax.shift_left(jnp.int32(1), shift)
            table_ref[owner, 0, rank] = h * EB + 1 + (block & (NB - 1))
            inverse_ref[owner, 0, rank] = r * HD * NB + i
            slot_ref[r * HD * NB + i] = jnp.where(
                rank < CAP, owner * CAP + rank, NS * CAP + rank - CAP
            )
            return (
                low + jnp.where(upper, 0, step),
                high + jnp.where(upper, step, 0),
                jnp.where(rank >= CAP, owner, hot),
            )

        carry = lax.fori_loop(0, HD * NB, one, carry, unroll=4)
    hot = carry[2]
    extra_ref[0] = hot
    for e in range(EXTRA):
        extra_ref[1 + e] = inverse_ref[hot, 0, CAP + e]


def request_table(ids):
    sm = spec(pltpu.SMEM)
    sds = jax.ShapeDtypeStruct
    tab = sds((NS, 1, 128), jnp.int32)
    return pl.pallas_call(
        table_kernel,
        name="request_table",
        out_shape=(tab, tab, sds((REQ,), jnp.int32), sds((8,), jnp.int32)),
        in_specs=[sm],
        out_specs=(sm, sm, sm, sm),
    )(ids)


def dot(a, b):
    return jnp.dot(a, b, preferred_element_type=jnp.float32)


def dot_nt(a, b):
    return lax.dot_general(a, b, (((1,), (1,)), ((), ())), preferred_element_type=jnp.float32)


def dot_tn(a, b):
    return lax.dot_general(a, b, (((0,), (0,)), ((), ())), preferred_element_type=jnp.float32)


def keep_rows(drops, h, j, half, low):
    d = [drops[h, n, j].astype(jnp.float32) * (1.0 / KEEP) for n in range(8)]
    if half == 0:
        ret = [jnp.where(low, d[0], d[1]), jnp.where(low, d[2], 0.0)]
    else:
        ret = [jnp.where(low, 0.0, d[0]), jnp.where(low, d[1], d[2])]
    ret += [jnp.where(low, d[3], d[4]), jnp.where(low, d[5], d[6])]
    return ret + [jnp.full((1, B), d[7], jnp.float32)]


COLS = ((0, 128), (128, 256), (256, 384), (384, 512), (512, 576))


def wide_sum(cols):
    return jnp.sum(cols[0] + cols[1] + cols[2] + cols[3], axis=1, keepdims=True) + jnp.sum(
        cols[4], axis=1, keepdims=True
    )


def main_kernel(
    q_in, k_in, v_in, g_in, table, inverse, slots, extra_s, drops, gids,
    att_out, dq_out, acc_out, ret_out, more_out, rim_out, gtot_out, wanted_out,
    kx, vx, qx, gx, kh, vh, sk, sv, rk, rv, probs, tk, tv, acck, accv, gacck, gaccv, att_v, dq_v,
    wanted_v, wanted_s, cand, cand_k, cand_v, chosen, glob, gsum, gpart, gdone, rim,
    first, pick_k, pick_v, second, last_k, last_v, back, back_in,
    send_x, recv_x, send_t, recv_t, local, send_r, recv_r, halo_s, halo_r, gl_s, gl_r, rim_s, rim_r, ex_s, ex_r,
):
    f32, bf = jnp.float32, jnp.bfloat16
    s = lax.axis_index("seq")
    hd = lax.axis_index("head")
    nxt = (s + 1) % NS
    prv = (s + NS - 1) % NS
    tail = pl.ds(0, NS - 1)

    def remote(src, dst, ssem, rsem, peer):
        pltpu.make_async_remote_copy(
            src, dst, ssem, rsem, device_id=(peer, hd), device_id_type=MESH
        ).start()

    def near(src, dst, sem):
        pltpu.make_async_copy(src, dst, sem).start()

    def drain(view, sem):
        pltpu.make_async_copy(view, view, sem).wait()

    def everyone(src, dst, ssem, rsem):
        for off in OFFS:
            p = seq_peer(s, off)
            remote(src(p), dst, ssem, rsem, p)
        near(src(s), dst, rsem)

    y, z = s % 4, s // 4
    hot = extra_s[0]
    hot_y, hot_z = lax.rem(hot, 4), lax.div(hot, 4)

    def axes(e):
        if e == 0:
            return y, z, hot_y, hot_z, lambda a, b: b * 4 + a
        return z, y, hot_z, hot_y, lambda a, b: a * 4 + b

    def ring(me):
        return [(me + n) % 4 for n in (1, 3, 2)]

    barrier = pltpu.get_barrier_semaphore()
    for off in OFFS:
        pl.semaphore_signal(barrier, inc=1, device_id=(seq_peer(s, off), hd), device_id_type=MESH)
    for dh in range(1, NH):
        pl.semaphore_signal(barrier, inc=1, device_id=(s, (hd + dh) % NH), device_id_type=MESH)
    pl.semaphore_wait(barrier, NS - 1 + NH - 1)

    def tiles(n):
        src, dst = ((k_in, kx), (v_in, vx))[n]
        for h in range(HD):
            for i in range(2):
                yield src, pl.ds(i * B, B), h, dst.at[h * EB + 1 + hd * 2 + i], n

    def rows(n):
        src, dst = ((q_in, qx), (g_in, gx))[n]
        for h in range(HD):
            at = pl.ds(pl.multiple_of(h * T + hd * 128, 128), 128)
            yield src, slice(None), h, dst.at[at, :], 2 + n

    def pieces(group):
        for src, at, h, dst, n in group:
            for dh in (1, 6, 7, 2, 3, 4, 5, 0):
                yield src, at, h, dst, n, dh

    def over_x(piece):
        src, at, h, dst, n, dh = piece
        p = (hd + dh) % NH
        a = src.at[at, pl.ds(pl.multiple_of((p * HD + h) * W, W), W)]
        if dh == 0:
            near(a, dst, recv_x.at[n])
        else:
            pltpu.make_async_remote_copy(
                a, dst, send_x, recv_x.at[n], device_id=(s, p), device_id_type=MESH
            ).start()

    for piece in pieces(tiles(0)):
        over_x(piece)
    everyone(lambda p: table.at[p], wanted_v.at[s], send_t, recv_t)
    later = list(pieces(tiles(1))) + list(pieces(rows(0))) + list(pieces(rows(1)))
    cuts = [0, 16, 32, 48, 64] + [64 + 8 * n for n in range(1, 8)] + [len(later)]

    drain(wanted_v, recv_t)
    to_scalar = pltpu.make_async_copy(wanted_v, wanted_s, local.at[0])
    to_scalar.start()
    near(wanted_v, wanted_out, local.at[1])
    to_scalar.wait()

    def spread_blocks(n, x, stage, landing, extra):
        halo = (kh, vh)[n]
        cand_in = (cand_k, cand_v)[n]
        for h in range(HD):
            remote(x.at[h * EB + NB], halo.at[0, h], halo_s.at[n], halo_r.at[n], nxt)
            remote(x.at[h * EB + 1], halo.at[1, h], halo_s.at[n], halo_r.at[n], prv)
        for gb in range(G):
            mine = jnp.clip(gids[gb] - s * NB, 0, NB - 1)
            for h in range(HD):
                tile = x[h * EB + 1 + mine]
                for half in range(2):
                    cand[n, h * 4 + gb * 2 + half] = tile[half * 32:half * 32 + 32]

        def gather(t):
            for m, off in enumerate(OFFS + ((0, 0),)):
                code = jnp.maximum(wanted_s[seq_peer(s, off), 0, t], 0)
                stage[m, t] = x[code]

        def send(t):
            for m, off in enumerate(OFFS):
                remote(
                    stage.at[m, t], landing.at[s * CAP + t], send_r.at[n], recv_r.at[n],
                    seq_peer(s, off),
                )
            near(stage.at[NS - 1, t], landing.at[s * CAP + t], recv_r.at[n])

        pick, last = ((pick_k, last_k), (pick_v, last_v))[n]
        for e in range(EXTRA):
            a, b, _, _, shard = axes(e)
            for j, to in enumerate([a] + ring(a)):
                for other in range(4):
                    code = jnp.maximum(wanted_s[shard(to, other), 0, CAP + e], 0)
                    first[n, e, j, other] = x[code]
        gather(0)
        for e in range(EXTRA):
            a, b, _, _, shard = axes(e)
            for j, to in enumerate(ring(a)):
                remote(
                    first.at[n, e, 1 + j], pick.at[pl.ds(e * 16 + a * 4, 4)],
                    ex_s.at[2 * n], ex_r.at[2 * n], shard(to, b),
                )
            near(first.at[n, e, 0], pick.at[pl.ds(e * 16 + a * 4, 4)], ex_r.at[2 * n])
        everyone(lambda p: cand.at[n, p], cand_in.at[s], gl_s.at[2 * n], gl_r.at[2 * n])
        for t in range(CAP):
            if t + 1 < CAP:
                gather(t + 1)
            send(t)
            for piece in later[cuts[t]:cuts[t + 1]] if extra else ():
                over_x(piece)
            if t == 5:
                drain(cand_in, gl_r.at[2 * n])
                owner = lax.div(gids[lax.rem(lax.div(s, 2), 2)], NB)
                chosen[n] = cand_in[owner]
                drain(pick, ex_r.at[2 * n])
                for e in range(EXTRA):
                    a, b, hot_a, _, shard = axes(e)
                    for j, to in enumerate([b] + ring(b)):
                        second[n, e, j] = pick[e * 16 + hot_a * 4 + to]
            if t == 6:
                for e in range(EXTRA):
                    a, b, _, _, shard = axes(e)
                    for j, to in enumerate(ring(b)):
                        remote(
                            second.at[n, e, 1 + j], last.at[e * 4 + b],
                            ex_s.at[2 * n + 1], ex_r.at[2 * n + 1], shard(a, to),
                        )
                    near(second.at[n, e, 0], last.at[e * 4 + b], ex_r.at[2 * n + 1])
                everyone(
                    lambda p: chosen.at[n], glob.at[n, s], gl_s.at[2 * n + 1], gl_r.at[2 * n + 1]
                )

    def await_blocks(n, x, landing):
        halo = (kh, vh)[n]
        drain(halo, halo_r.at[n])
        for h in range(HD):
            x[h * EB] = halo[0, h]
            x[h * EB + NB + 1] = halo[1, h]
        drain(glob.at[n], gl_r.at[2 * n + 1])
        drain(landing.at[pl.ds(0, NS * CAP)], recv_r.at[n])
        last = (last_k, last_v)[n]
        drain(last, ex_r.at[2 * n + 1])
        for e in range(EXTRA):
            hot_b = axes(e)[3]
            landing[NS * CAP + e] = last[e * 4 + hot_b]

    drain(kx.at[pl.ds(0, HD * NB)], recv_x.at[0])
    spread_blocks(0, kx, sk, rk, True)
    drain(vx.at[pl.ds(0, HD * NB)], recv_x.at[1])
    spread_blocks(1, vx, sv, rv, False)

    accv[...] = jnp.zeros_like(accv)
    acck[...] = jnp.zeros_like(acck)
    gaccv[...] = jnp.zeros_like(gaccv)
    gacck[...] = jnp.zeros_like(gacck)
    drain(qx, recv_x.at[2])
    drain(gx, recv_x.at[3])
    await_blocks(0, kx, rk)

    low = lax.broadcasted_iota(jnp.int32, (1, W), 1) < B
    low2 = lax.broadcasted_iota(jnp.int32, (B, W), 1) < B
    ninf = f32(-jnp.inf)

    def place(i):
        h = lax.div(i, NB // 2)
        p = lax.rem(i, NB // 2)
        at = pl.ds(pl.multiple_of(i * 2 * B, 2 * B), 2 * B)
        ext = pl.ds(pl.multiple_of(p * 2 * B, 2 * B), 4 * B)
        return h, p, at, ext

    def listed(n, x, landing, h, p):
        window = x[pl.ds(h * EB + 2 * p, 4)].reshape(4 * B, W)
        wide = glob[n, pl.ds(h * 4, 4)].reshape(2 * B, W)
        rand = []
        for half in range(2):
            own = [landing[slots[r * HD * NB + h * NB + 2 * p + half]] for r in range(R)]
            rand.append(jnp.concatenate(own, 0))
        return jnp.concatenate([window, wide], 0), rand

    def store_terms(term, h, p, half, tiles):
        for r in range(R):
            term[r * HD * NB + h * NB + 2 * p + half] = tiles[r * B:(r + 1) * B]

    def phase1(i, c):
        h, p, at, ext = place(i)
        q = qx[at, :]
        g = gx[at, :]
        kwg, kr = listed(0, kx, rk, h, p)
        swg = dot_nt(q, kwg)
        pds = []
        for half in range(2):
            hb = slice(half * B, (half + 1) * B)
            sr = dot_nt(q[hb], kr[half])
            c0, c1, c2 = (swg[hb, n * W:(n + 1) * W] for n in range(3))
            absent0 = jnp.logical_and(s == 0, p == 0) if half == 0 else True
            absent3 = jnp.logical_and(s == NS - 1, p == NB // 2 - 1) if half == 1 else True
            c0 = jnp.where(jnp.logical_and(low2, absent0), ninf, c0)
            c1 = jnp.where(jnp.logical_and(jnp.logical_not(low2), absent3), ninf, c1)
            cols = [c0, c1, c2, sr[:, :W], sr[:, W:]]
            top = jnp.maximum(jnp.maximum(c0, c1), jnp.maximum(c2, cols[3]))
            top = jnp.maximum(
                jnp.max(top, axis=1, keepdims=True), jnp.max(cols[4], axis=1, keepdims=True)
            )
            e = [jnp.exp2((x - top) * (SCALE * LOG2E)) for x in cols]
            inv = 1.0 / wide_sum(e)
            pr = [x * inv for x in e]
            for (a, b), x in zip(COLS, pr):
                probs[i, hb, a:b] = x
            ret = keep_rows(drops, h, 2 * p + half, half, low)
            pds.append([(x * y).astype(bf) for x, y in zip(pr, ret)])
        pd_wg = jnp.concatenate([jnp.concatenate(x[:3], 1) for x in pds], 0)
        dv = dot_tn(pd_wg, g)
        accv[h, ext, :] += dv[:4 * B]
        gaccv[h] += dv[4 * B:]
        for half in range(2):
            dvr = dot_tn(jnp.concatenate(pds[half][3:], 1), g[half * B:(half + 1) * B])
            store_terms(tv, h, p, half, dvr.astype(bf))
        return c

    def phase2(i, c):
        h, p, at, ext = place(i)
        q = qx[at, :]
        g = gx[at, :]
        kwg, kr = listed(0, kx, rk, h, p)
        vwg, vr = listed(1, vx, rv, h, p)
        dwg = dot_nt(g, vwg)
        halves = []
        for half in range(2):
            hb = slice(half * B, (half + 1) * B)
            dr = dot_nt(g[hb], vr[half])
            raw = [dwg[hb, n * W:(n + 1) * W] for n in range(3)] + [dr[:, :W], dr[:, W:]]
            pr = [probs[i, hb, a:b] for a, b in COLS]
            ret = keep_rows(drops, h, 2 * p + half, half, low)
            dp = [x * y for x, y in zip(raw, ret)]
            delta = wide_sum([x * y for x, y in zip(pr, dp)])
            pd = [(x * y).astype(bf) for x, y in zip(pr, ret)]
            ds = [(x * (y - delta)).astype(bf) for x, y in zip(pr, dp)]
            halves.append((pd, ds))
        pd_wg = jnp.concatenate([jnp.concatenate(x[0][:3], 1) for x in halves], 0)
        ds_wg = jnp.concatenate([jnp.concatenate(x[1][:3], 1) for x in halves], 0)
        pd_r = [jnp.concatenate(x[0][3:], 1) for x in halves]
        ds_r = [jnp.concatenate(x[1][3:], 1) for x in halves]
        att = dot(pd_wg, vwg) + jnp.concatenate([dot(a, b) for a, b in zip(pd_r, vr)], 0)
        att_v[at, :] = att.astype(bf)
        dq = dot(ds_wg, kwg) + jnp.concatenate([dot(a, b) for a, b in zip(ds_r, kr)], 0)
        dq_v[at, :] = (dq * SCALE).astype(bf)
        dk = dot_tn(ds_wg, q) * SCALE
        acck[h, ext, :] += dk[:4 * B]
        gacck[h] += dk[4 * B:]
        for half in range(2):
            dkr = dot_tn(ds_r[half], q[half * B:(half + 1) * B]) * SCALE
            store_terms(tk, h, p, half, dkr.astype(bf))
        return c

    def give_back(n, m, acc, gacc, term, stage):
        for h in range(HD):
            rim[n, 0, h] = acc[h, :B].astype(bf)
            rim[n, 1, h] = acc[h, B + T:].astype(bf)
            for c in range(4):
                gsum[n, h * 4 + c] = gacc[h, c * 32:(c + 1) * 32].astype(bf)
        near(acc, acc_out.at[n], local.at[2 + n])

        def gather(t):
            for j, off in enumerate(OFFS + ((0, 0),)):
                stage[j, t] = term[inverse[seq_peer(s, off), 0, t]]

        def send(t):
            for j, off in enumerate(OFFS):
                remote(
                    stage.at[j, t], ret_out.at[n, s, t], send_r.at[m], recv_r.at[m],
                    seq_peer(s, off),
                )
            near(stage.at[NS - 1, t], ret_out.at[n, s, t], recv_r.at[m])

        for e in range(EXTRA):
            back[n, e] = term[extra_s[1 + e]]
        gather(0)
        for e in range(EXTRA):
            a, b, _, _, shard = axes(e)
            for to in ring(b):
                remote(
                    back.at[n, e], back_in.at[n, e, b], ex_s.at[2 * m], ex_r.at[2 * m],
                    shard(a, to),
                )
            near(back.at[n, e], back_in.at[n, e, b], ex_r.at[2 * m])
        everyone(lambda p: gsum.at[n, p], gpart.at[n, s], gl_s.at[2 * m], gl_r.at[2 * m])
        remote(rim.at[n, 0], rim_out.at[n, 1], rim_s.at[n], rim_r.at[n], prv)
        remote(rim.at[n, 1], rim_out.at[n, 0], rim_s.at[n], rim_r.at[n], nxt)
        for t in range(CAP):
            if t + 1 < CAP:
                gather(t + 1)
            send(t)
            if t == 5:
                drain(gpart.at[n], gl_r.at[2 * m])
                total = gpart[n, 0].astype(f32)
                for i in range(1, NS):
                    total = total + gpart[n, i].astype(f32)
                gdone[n] = total.astype(bf)
                drain(back_in.at[n], ex_r.at[2 * m])
                for e in range(EXTRA):
                    a, b, _, _, shard = axes(e)
                    for to in ring(a):
                        remote(
                            back_in.at[n, e], more_out.at[n, e, a], ex_s.at[2 * m + 1],
                            ex_r.at[2 * m + 1], shard(to, b),
                        )
                    near(back_in.at[n, e], more_out.at[n, e, a], ex_r.at[2 * m + 1])
            if t == 6:
                everyone(
                    lambda p: gdone.at[n], gtot_out.at[n, s], gl_s.at[2 * m + 1],
                    gl_r.at[2 * m + 1],
                )

    lax.fori_loop(0, HD * NB // 2, phase1, 0)
    drain(sk.at[tail], send_r.at[0])
    give_back(1, 2, accv, gaccv, tv, sk)
    await_blocks(1, vx, rv)
    lax.fori_loop(0, HD * NB // 2, phase2, 0)
    drain(sv.at[tail], send_r.at[1])
    give_back(0, 3, acck, gacck, tk, sv)
    for h in range(HD):
        near(att_v.at[pl.ds(h * T, T), :], att_out.at[:, pl.ds(h * W, W)], local.at[4])
        near(dq_v.at[pl.ds(h * T, T), :], dq_out.at[:, pl.ds(h * W, W)], local.at[5])

    drain(wanted_v, local.at[1])
    drain(wanted_v.at[tail], send_t)
    drain(probs.at[pl.ds(0, 28), :, pl.ds(0, 256)], send_x)
    for n in range(2):
        drain(kh, halo_s.at[n])
        drain(rim.at[n], rim_s.at[n])
        drain(rim_out.at[n], rim_r.at[n])
        drain((acck, accv)[n], local.at[2 + n])
    for m in range(8):
        drain(glob.at[0, tail], gl_s.at[m])
    for n in range(2):
        step1 = first.at[n, :, pl.ds(0, 3)]
        step2 = second.at[n, :, pl.ds(0, 3)]
        drain(step1, ex_s.at[2 * n])
        drain(step2, ex_s.at[2 * n + 1])
        drain(step2, ex_s.at[4 + 2 * n])
        drain(step1, ex_s.at[5 + 2 * n])
        drain(more_out.at[n], ex_r.at[7 - 2 * n])
    drain(gtot_out.at[1], gl_r.at[5])
    drain(gtot_out.at[0], gl_r.at[7])
    drain(att_v, local.at[4])
    drain(dq_v, local.at[5])
    drain(sk.at[tail], send_r.at[2])
    drain(ret_out.at[1], recv_r.at[2])
    drain(sv.at[tail], send_r.at[3])
    drain(ret_out.at[0], recv_r.at[3])


def main_call(q, k, v, g, table, inverse, slots, extra, drops, gids):
    bf, f32 = jnp.bfloat16, jnp.float32
    sds = jax.ShapeDtypeStruct
    dma = pltpu.SemaphoreType.DMA
    sm = spec(pltpu.SMEM)
    tile = (B, W)
    chunk = (NS, 32, W)
    return pl.pallas_call(
        main_kernel,
        name="exchange_attend",
        out_shape=(
            sds((T, HD * W), bf), sds((T, HD * W), bf), sds((2, HD, EB * B, W), f32),
            sds((2, NS, CAP) + tile, bf), sds((2, EXTRA, 4, 4) + tile, bf), sds((2, 2, HD) + tile, bf), sds((2,) + chunk, bf),
            sds((NS, 1, 128), jnp.int32),
        ),
        in_specs=[spec(ANY)] * 5 + [sm] * 5,
        out_specs=(spec(ANY),) * 8,
        scratch_shapes=[
            VM((HD * EB,) + tile, bf), VM((HD * EB,) + tile, bf),
            VM((HD * T, W), bf), VM((HD * T, W), bf),
            VM((2, HD) + tile, bf), VM((2, HD) + tile, bf),
            VM((NS, CAP) + tile, bf), VM((NS, CAP) + tile, bf),
            VM((NS * CAP + EXTRA,) + tile, bf), VM((NS * CAP + EXTRA,) + tile, bf),
            VM((HD * NB // 2, 2 * B, 640), f32),
            VM((REQ,) + tile, bf), VM((REQ,) + tile, bf),
            VM((HD, EB * B, W), f32), VM((HD, EB * B, W), f32),
            VM((HD, 2 * B, W), f32), VM((HD, 2 * B, W), f32),
            VM((HD * T, W), bf), VM((HD * T, W), bf),
            VM((NS, 1, 128), jnp.int32), pltpu.SMEM((NS, 1, 128), jnp.int32),
            VM((2,) + chunk, bf), VM(chunk, bf), VM(chunk, bf), VM((2, 32, W), bf), VM((2,) + chunk, bf),
            VM((2,) + chunk, bf), VM((2,) + chunk, bf), VM((2, 32, W), bf),
            VM((2, 2, HD) + tile, bf),
            VM((2, EXTRA, 4, 4) + tile, bf), VM((EXTRA * 16,) + tile, bf), VM((EXTRA * 16,) + tile, bf),
            VM((2, EXTRA, 4) + tile, bf), VM((EXTRA * 4,) + tile, bf), VM((EXTRA * 4,) + tile, bf),
            VM((2, EXTRA) + tile, bf), VM((2, EXTRA, 4) + tile, bf),
            dma, dma((4,)), dma, dma, dma((6,)), dma((4,)), dma((4,)),
            dma((2,)), dma((2,)), dma((8,)), dma((8,)), dma((2,)), dma((2,)), dma((8,)), dma((8,)),
        ],
        compiler_params=pltpu.CompilerParams(
            collective_id=0, has_side_effects=True, vmem_limit_bytes=VLIM
        ),
    )(q, k, v, g, table, inverse, slots, extra, drops, gids)


def gather_up_kernel(
    wanted, gids, shard, extra, acc_in, rim, gtot, ret, more, att_in, dq_in, dk_ref, dv_ref, att_ref, dq_ref, acc
):
    s = shard[0]
    i = pl.program_id(0)
    f32 = jnp.float32
    att_ref[...] = att_in[...]
    dq_ref[...] = dq_in[...]
    for h in range(HD):
        for b in range(NB):
            at = slice((b + 1) * B, (b + 2) * B)
            acc[h * EB + 1 + b] = acc_in[0, h, at]

        @pl.when(s > 0)
        def _():
            acc[h * EB + 1] += rim[0, 0, h].astype(f32)

        @pl.when(s < NS - 1)
        def _():
            acc[h * EB + NB] += rim[0, 1, h].astype(f32)

        for gb in range(G):
            mine = gids[gb] - s * NB

            @pl.when(jnp.logical_and(mine >= 0, mine < NB))
            def _():
                acc[h * EB + 1 + mine] += gtot[0, pl.ds(h * 4 + gb * 2, 2)].reshape(B, W).astype(f32)

    def add(lister, c):
        for t in range(CAP):
            code = wanted[lister, 0, t]
            at = jnp.where(code < 0, HD * EB, code)
            acc[at] += ret[0, lister, t].astype(f32)
        return c

    lax.fori_loop(0, NS, add, 0)

    @pl.when(s == extra[0])
    def _():
        for e in range(EXTRA):
            for a in range(4):
                for b in range(4):
                    code = wanted[b * 4 + a if e == 0 else a * 4 + b, 0, CAP + e]
                    at = jnp.where(code < 0, HD * EB, code)
                    acc[at] += more[0, e, a, b].astype(f32)

    for n, out in enumerate((dk_ref, dv_ref)):

        @pl.when(i == n)
        def _():
            for h in range(HD):
                for b in range(NB):
                    out[b * B:(b + 1) * B, h * W:(h + 1) * W] = acc[h * EB + 1 + b].astype(jnp.bfloat16)


def gather_up(wanted, gids, shard, extra, acc, rim, gtot, ret, more, att, dq):
    sds = jax.ShapeDtypeStruct
    sm = spec(pltpu.SMEM)
    whole = pl.BlockSpec((T, HD * W), lambda i: (0, 0))
    part = pl.BlockSpec((T // 2, HD * W), lambda i: (i, 0))
    return pl.pallas_call(
        gather_up_kernel,
        name="gather_up",
        grid=(2,),
        out_shape=(sds((T, HD * W), jnp.bfloat16),) * 4,
        in_specs=[
            sm, sm, sm, sm,
            pl.BlockSpec((1, HD, EB * B, W), lambda i: (i, 0, 0, 0)),
            pl.BlockSpec((1, 2, HD, B, W), lambda i: (i, 0, 0, 0, 0)),
            pl.BlockSpec((1, NS, 32, W), lambda i: (i, 0, 0, 0)),
            pl.BlockSpec((1, NS, CAP, B, W), lambda i: (i, 0, 0, 0, 0)),
            pl.BlockSpec((1, EXTRA, 4, 4, B, W), lambda i: (i, 0, 0, 0, 0, 0)),
            part, part,
        ],
        out_specs=(whole, whole, part, part),
        scratch_shapes=[VM((HD * EB + 1, B, W), jnp.float32)],
        compiler_params=pltpu.CompilerParams(vmem_limit_bytes=VLIM),
    )(wanted, gids, shard, extra, acc, rim, gtot, ret, more, att, dq)


def per_device(queries, keys, values, grad_out, rand_blocks, global_ids, drop_mask):
    shard = lax.axis_index("seq").astype(jnp.int32).reshape(1)
    table, inverse, slots, extra = request_table(rand_blocks.transpose(2, 0, 1))
    att, dq, acc, ret, more, rim, gtot, wanted = main_call(
        queries, keys, values, grad_out, table, inverse, slots, extra,
        drop_mask.transpose(0, 2, 1), global_ids,
    )
    dk, dv, att, dq = gather_up(
        wanted, global_ids, shard, extra, acc, rim, gtot, ret, more, att, dq
    )
    return att, dq, dk, dv


def solution(mesh):
    rows = P(("seq", "head"), None)
    out = P("seq", "head")
    return jax.shard_map(
        per_device,
        mesh=mesh,
        in_specs=(rows, rows, rows, rows, P("head", "seq", None), P(), P("head", "seq", None)),
        out_specs=(out, out, out, out),
        check_vma=False,
    )
```

```python
import functools
import math

import jax
import jax.numpy as jnp
from jax import lax
from jax.experimental import pallas as pl
from jax.experimental.pallas import tpu as pltpu
from jax.sharding import PartitionSpec as P

W = 128
B = 64
R = 3
G = 2
NS = 16
NH = 8
HD = 4
NB = 16
EB = NB + 2
CAP = 12
CUT = 16
EXTRA = 3
REQ = HD * NB * R
T = NB * B
KEEP = 0.9
SCALE = W**-0.5
LOG2E = math.log2(math.e)
MESH = pl.DeviceIdType.MESH
VM = pltpu.VMEM
ANY = pl.ANY
VLIM = 62 * 1024 * 1024

OFFS = (
    (0, 1), (1, 0), (0, 3), (3, 0), (0, 2), (2, 0), (1, 1), (3, 3),
    (1, 3), (3, 1), (1, 2), (2, 1), (3, 2), (2, 3), (2, 2),
)


def seq_peer(s, off):
    return ((s // 4 + off[0]) % 4) * 4 + (s % 4 + off[1]) % 4


def spec(space):
    return pl.BlockSpec(memory_space=space)


def table_kernel(ids_ref, table_ref, inverse_ref, slot_ref, extra_ref):
    def clear(i, c):
        for o in range(NS):
            table_ref[o, 0, i] = -1
            inverse_ref[o, 0, i] = 0
        return c

    lax.fori_loop(0, CAP + EXTRA, clear, 0)
    carry = (jnp.int32(0), jnp.int32(0), jnp.int32(0))
    for r in range(R):

        def one(i, carry):
            low, high, hot = carry
            h = lax.shift_right_logical(i, 4)
            block = ids_ref[r, h, i & (NB - 1)]
            owner = lax.shift_right_logical(block, 4)
            shift = (owner & 7) * 4
            upper = owner >= NS // 2
            rank = lax.shift_right_logical(jnp.where(upper, high, low), shift) & 15
            step = lax.shift_left(jnp.int32(1), shift)
            table_ref[owner, 0, rank] = h * EB + 1 + (block & (NB - 1))
            inverse_ref[owner, 0, rank] = r * HD * NB + i
            slot_ref[r * HD * NB + i] = jnp.where(
                rank < CAP, owner * CAP + rank, NS * CAP + rank - CAP
            )
            return (
                low + jnp.where(upper, 0, step),
                high + jnp.where(upper, step, 0),
                jnp.where(rank >= CAP, owner, hot),
            )

        carry = lax.fori_loop(0, HD * NB, one, carry, unroll=4)
    hot = carry[2]
    extra_ref[0] = hot
    for e in range(EXTRA):
        extra_ref[1 + e] = inverse_ref[hot, 0, CAP + e]


def request_table(ids):
    sm = spec(pltpu.SMEM)
    sds = jax.ShapeDtypeStruct
    tab = sds((NS, 1, 128), jnp.int32)
    return pl.pallas_call(
        table_kernel,
        name="request_table",
        out_shape=(tab, tab, sds((REQ,), jnp.int32), sds((8,), jnp.int32)),
        in_specs=[sm],
        out_specs=(sm, sm, sm, sm),
    )(ids)


def dot(a, b):
    return jnp.dot(a, b, preferred_element_type=jnp.float32)


def dot_nt(a, b):
    return lax.dot_general(a, b, (((1,), (1,)), ((), ())), preferred_element_type=jnp.float32)


def dot_tn(a, b):
    return lax.dot_general(a, b, (((0,), (0,)), ((), ())), preferred_element_type=jnp.float32)


def keep_rows(drops, h, j, half, low):
    d = [drops[h, n, j].astype(jnp.float32) * (1.0 / KEEP) for n in range(8)]
    if half == 0:
        ret = [jnp.where(low, d[0], d[1]), jnp.where(low, d[2], 0.0)]
    else:
        ret = [jnp.where(low, 0.0, d[0]), jnp.where(low, d[1], d[2])]
    ret += [jnp.where(low, d[3], d[4]), jnp.where(low, d[5], d[6])]
    return ret + [jnp.full((1, B), d[7], jnp.float32)]


COLS = ((0, 128), (128, 256), (256, 384), (384, 512), (512, 576))


def wide_sum(cols):
    return jnp.sum(cols[0] + cols[1] + cols[2] + cols[3], axis=1, keepdims=True) + jnp.sum(
        cols[4], axis=1, keepdims=True
    )


def main_kernel(
    q_in, k_in, v_in, g_in, table, inverse, slots, extra_s, drops, gids,
    att_out, dq_out, acc_out, ret_out, more_out, rim_out, gtot_out, wanted_out,
    ka, kb, vx, qx, gx, kh, vh, sk, sv, rk, rv, probs, tk, tv, acck, accv, gacck, gaccv, att_v, dq_v,
    wanted_v, wanted_s, cand, cand_k, cand_v, chosen, glob, gsum, gpart, gdone, rim,
    first, pick_k, pick_v, second, last_k, last_v, back, back_in,
    send_x, recv_x, send_t, recv_t, local, send_r, recv_r, halo_s, halo_r, gl_s, gl_r, rim_s, rim_r, ex_s, ex_r,
):
    f32, bf = jnp.float32, jnp.bfloat16
    s = lax.axis_index("seq")
    hd = lax.axis_index("head")
    nxt = (s + 1) % NS
    prv = (s + NS - 1) % NS
    tail = pl.ds(0, NS - 1)

    def remote(src, dst, ssem, rsem, peer):
        pltpu.make_async_remote_copy(
            src, dst, ssem, rsem, device_id=(peer, hd), device_id_type=MESH
        ).start()

    def near(src, dst, sem):
        pltpu.make_async_copy(src, dst, sem).start()

    def drain(view, sem):
        pltpu.make_async_copy(view, view, sem).wait()

    def everyone(src, dst, ssem, rsem):
        for off in OFFS:
            p = seq_peer(s, off)
            remote(src(p), dst, ssem, rsem, p)
        near(src(s), dst, rsem)

    y, z = s % 4, s // 4
    hot = extra_s[0]
    hot_y, hot_z = lax.rem(hot, 4), lax.div(hot, 4)

    def axes(e):
        if e == 0:
            return y, z, hot_y, hot_z, lambda a, b: b * 4 + a
        return z, y, hot_z, hot_y, lambda a, b: a * 4 + b

    def ring(me):
        return [(me + n) % 4 for n in (1, 3, 2)]

    barrier = pltpu.get_barrier_semaphore()
    for off in OFFS:
        pl.semaphore_signal(barrier, inc=1, device_id=(seq_peer(s, off), hd), device_id_type=MESH)
    for dh in range(1, NH):
        pl.semaphore_signal(barrier, inc=1, device_id=(s, (hd + dh) % NH), device_id_type=MESH)
    pl.semaphore_wait(barrier, NS - 1 + NH - 1)

    def key_tiles(half):
        for h in range(HD):
            for i in range(2):
                at = pl.ds(i * B + half * CUT, (CUT, B - CUT)[half])
                yield k_in, at, h, (ka, kb)[half].at[h * EB + 1 + hd * 2 + i], 4 * half

    def value_tiles():
        for h in range(HD):
            for i in range(2):
                yield v_in, pl.ds(i * B, B), h, vx.at[h * EB + 1 + hd * 2 + i], 1

    def rows(n):
        src, dst = ((q_in, qx), (g_in, gx))[n]
        for h in range(HD):
            at = pl.ds(pl.multiple_of(h * T + hd * 128, 128), 128)
            yield src, slice(None), h, dst.at[at, :], 2 + n

    def pieces(group):
        for src, at, h, dst, n in group:
            for dh in (1, 6, 7, 2, 3, 4, 5, 0):
                yield src, at, h, dst, n, dh

    def over_x(piece):
        src, at, h, dst, n, dh = piece
        p = (hd + dh) % NH
        a = src.at[at, pl.ds(pl.multiple_of((p * HD + h) * W, W), W)]
        if dh == 0:
            near(a, dst, recv_x.at[n])
        else:
            pltpu.make_async_remote_copy(
                a, dst, send_x, recv_x.at[n], device_id=(s, p), device_id_type=MESH
            ).start()

    for half in range(2):
        for piece in pieces(key_tiles(half)):
            over_x(piece)
    everyone(lambda p: table.at[p], wanted_v.at[s], send_t, recv_t)
    later = list(pieces(value_tiles())) + list(pieces(rows(0))) + list(pieces(rows(1)))
    cuts = [0, 16, 32, 48, 64] + [64 + 8 * n for n in range(1, 8)] + [len(later)]

    drain(wanted_v, recv_t)
    to_scalar = pltpu.make_async_copy(wanted_v, wanted_s, local.at[0])
    to_scalar.start()
    near(wanted_v, wanted_out, local.at[1])
    to_scalar.wait()

    def spread_blocks(n, xs, arrive, stage, landing, extra):
        halo = (kh, vh)[n]
        cand_in = (cand_k, cand_v)[n]
        pick, last = ((pick_k, last_k), (pick_v, last_v))[n]
        spans = ((0, B),) if len(xs) == 1 else ((0, CUT), (CUT, B))

        def gather(t, i):
            for m, off in enumerate(OFFS + ((0, 0),)):
                code = jnp.maximum(wanted_s[seq_peer(s, off), 0, t], 0)
                stage[m, t, spans[i][0]:spans[i][1]] = xs[i][code]

        def send(t, i):
            part = pl.ds(spans[i][0], spans[i][1] - spans[i][0])
            for m, off in enumerate(OFFS):
                remote(
                    stage.at[m, t, part], landing.at[s * CAP + t, part], send_r.at[n],
                    recv_r.at[n], seq_peer(s, off),
                )
            near(stage.at[NS - 1, t, part], landing.at[s * CAP + t, part], recv_r.at[n])

        if len(xs) == 2:
            arrive[0]()
            gather(0, 0)
            for t in range(CAP):
                if t + 1 < CAP:
                    gather(t + 1, 0)
                send(t, 0)
        final = len(xs) - 1
        arrive[final]()
        for h in range(HD):
            for i, x in enumerate(xs):
                part = pl.ds(spans[i][0], spans[i][1] - spans[i][0])
                remote(x.at[h * EB + NB], halo.at[0, h, part], halo_s.at[n], halo_r.at[n], nxt)
                remote(x.at[h * EB + 1], halo.at[1, h, part], halo_s.at[n], halo_r.at[n], prv)
        for gb in range(G):
            mine = jnp.clip(gids[gb] - s * NB, 0, NB - 1)
            for h in range(HD):
                tile = jnp.concatenate([x[h * EB + 1 + mine] for x in xs], 0)
                for half in range(2):
                    cand[n, h * 4 + gb * 2 + half] = tile[half * 32:half * 32 + 32]
        for e in range(EXTRA):
            a, b, _, _, shard = axes(e)
            for j, to in enumerate([a] + ring(a)):
                for other in range(4):
                    code = jnp.maximum(wanted_s[shard(to, other), 0, CAP + e], 0)
                    for i, x in enumerate(xs):
                        first[n, e, j, other, spans[i][0]:spans[i][1]] = x[code]
        gather(0, final)
        for e in range(EXTRA):
            a, b, _, _, shard = axes(e)
            for j, to in enumerate(ring(a)):
                remote(
                    first.at[n, e, 1 + j], pick.at[pl.ds(e * 16 + a * 4, 4)],
                    ex_s.at[2 * n], ex_r.at[2 * n], shard(to, b),
                )
            near(first.at[n, e, 0], pick.at[pl.ds(e * 16 + a * 4, 4)], ex_r.at[2 * n])
        everyone(lambda p: cand.at[n, p], cand_in.at[s], gl_s.at[2 * n], gl_r.at[2 * n])
        for t in range(CAP):
            if t + 1 < CAP:
                gather(t + 1, final)
            send(t, final)
            for piece in later[cuts[t]:cuts[t + 1]] if extra else ():
                over_x(piece)
            if t == 5:
                drain(cand_in, gl_r.at[2 * n])
                owner = lax.div(gids[lax.rem(lax.div(s, 2), 2)], NB)
                chosen[n] = cand_in[owner]
                drain(pick, ex_r.at[2 * n])
                for e in range(EXTRA):
                    a, b, hot_a, _, shard = axes(e)
                    for j, to in enumerate([b] + ring(b)):
                        second[n, e, j] = pick[e * 16 + hot_a * 4 + to]
            if t == 6:
                for e in range(EXTRA):
                    a, b, _, _, shard = axes(e)
                    for j, to in enumerate(ring(b)):
                        remote(
                            second.at[n, e, 1 + j], last.at[e * 4 + b],
                            ex_s.at[2 * n + 1], ex_r.at[2 * n + 1], shard(a, to),
                        )
                    near(second.at[n, e, 0], last.at[e * 4 + b], ex_r.at[2 * n + 1])
                everyone(
                    lambda p: chosen.at[n], glob.at[n, s], gl_s.at[2 * n + 1], gl_r.at[2 * n + 1]
                )

    def await_blocks(n, xs, landing):
        halo = (kh, vh)[n]
        drain(halo, halo_r.at[n])
        for h in range(HD):
            for x, (i, j) in zip(xs, ((0, B),) if len(xs) == 1 else ((0, CUT), (CUT, B))):
                x[h * EB] = halo[0, h, i:j]
                x[h * EB + NB + 1] = halo[1, h, i:j]
        drain(glob.at[n], gl_r.at[2 * n + 1])
        drain(landing.at[pl.ds(0, NS * CAP)], recv_r.at[n])
        last = (last_k, last_v)[n]
        drain(last, ex_r.at[2 * n + 1])
        for e in range(EXTRA):
            hot_b = axes(e)[3]
            landing[NS * CAP + e] = last[e * 4 + hot_b]

    def arrival(x, sem):
        return lambda: drain(x.at[pl.ds(0, HD * NB)], sem)

    keys, values = (ka, kb), (vx,)
    spread_blocks(0, keys, (arrival(ka, recv_x.at[0]), arrival(kb, recv_x.at[4])), sk, rk, True)
    spread_blocks(1, values, (arrival(vx, recv_x.at[1]),), sv, rv, False)

    accv[...] = jnp.zeros_like(accv)
    acck[...] = jnp.zeros_like(acck)
    gaccv[...] = jnp.zeros_like(gaccv)
    gacck[...] = jnp.zeros_like(gacck)
    drain(qx, recv_x.at[2])
    drain(gx, recv_x.at[3])
    await_blocks(0, keys, rk)

    low = lax.broadcasted_iota(jnp.int32, (1, W), 1) < B
    low2 = lax.broadcasted_iota(jnp.int32, (B, W), 1) < B
    ninf = f32(-jnp.inf)

    def place(i):
        h = lax.div(i, NB // 2)
        p = lax.rem(i, NB // 2)
        at = pl.ds(pl.multiple_of(i * 2 * B, 2 * B), 2 * B)
        ext = pl.ds(pl.multiple_of(p * 2 * B, 2 * B), 4 * B)
        return h, p, at, ext

    def listed(n, xs, landing, h, p):
        window = [x[pl.ds(h * EB + 2 * p, 4)] for x in xs]
        window = jnp.concatenate(window, 1).reshape(4 * B, W)
        wide = glob[n, pl.ds(h * 4, 4)].reshape(2 * B, W)
        rand = []
        for half in range(2):
            own = [landing[slots[r * HD * NB + h * NB + 2 * p + half]] for r in range(R)]
            rand.append(jnp.concatenate(own, 0))
        return jnp.concatenate([window, wide], 0), rand

    def store_terms(term, h, p, half, tiles):
        for r in range(R):
            term[r * HD * NB + h * NB + 2 * p + half] = tiles[r * B:(r + 1) * B]

    def phase1(i, c):
        h, p, at, ext = place(i)
        q = qx[at, :]
        g = gx[at, :]
        kwg, kr = listed(0, keys, rk, h, p)
        swg = dot_nt(q, kwg)
        pds = []
        for half in range(2):
            hb = slice(half * B, (half + 1) * B)
            sr = dot_nt(q[hb], kr[half])
            c0, c1, c2 = (swg[hb, n * W:(n + 1) * W] for n in range(3))
            absent0 = jnp.logical_and(s == 0, p == 0) if half == 0 else True
            absent3 = jnp.logical_and(s == NS - 1, p == NB // 2 - 1) if half == 1 else True
            c0 = jnp.where(jnp.logical_and(low2, absent0), ninf, c0)
            c1 = jnp.where(jnp.logical_and(jnp.logical_not(low2), absent3), ninf, c1)
            cols = [c0, c1, c2, sr[:, :W], sr[:, W:]]
            top = jnp.maximum(jnp.maximum(c0, c1), jnp.maximum(c2, cols[3]))
            top = jnp.maximum(
                jnp.max(top, axis=1, keepdims=True), jnp.max(cols[4], axis=1, keepdims=True)
            )
            e = [jnp.exp2((x - top) * (SCALE * LOG2E)) for x in cols]
            inv = 1.0 / wide_sum(e)
            pr = [x * inv for x in e]
            for (a, b), x in zip(COLS, pr):
                probs[i, hb, a:b] = x
            ret = keep_rows(drops, h, 2 * p + half, half, low)
            pds.append([(x * y).astype(bf) for x, y in zip(pr, ret)])
        pd_wg = jnp.concatenate([jnp.concatenate(x[:3], 1) for x in pds], 0)
        dv = dot_tn(pd_wg, g)
        accv[h, ext, :] += dv[:4 * B]
        gaccv[h] += dv[4 * B:]
        for half in range(2):
            dvr = dot_tn(jnp.concatenate(pds[half][3:], 1), g[half * B:(half + 1) * B])
            store_terms(tv, h, p, half, dvr.astype(bf))
        return c

    def phase2(i, c):
        h, p, at, ext = place(i)
        q = qx[at, :]
        g = gx[at, :]
        kwg, kr = listed(0, keys, rk, h, p)
        vwg, vr = listed(1, values, rv, h, p)
        dwg = dot_nt(g, vwg)
        halves = []
        for half in range(2):
            hb = slice(half * B, (half + 1) * B)
            dr = dot_nt(g[hb], vr[half])
            raw = [dwg[hb, n * W:(n + 1) * W] for n in range(3)] + [dr[:, :W], dr[:, W:]]
            pr = [probs[i, hb, a:b] for a, b in COLS]
            ret = keep_rows(drops, h, 2 * p + half, half, low)
            dp = [x * y for x, y in zip(raw, ret)]
            delta = wide_sum([x * y for x, y in zip(pr, dp)])
            pd = [(x * y).astype(bf) for x, y in zip(pr, ret)]
            ds = [(x * (y - delta)).astype(bf) for x, y in zip(pr, dp)]
            halves.append((pd, ds))
        pd_wg = jnp.concatenate([jnp.concatenate(x[0][:3], 1) for x in halves], 0)
        ds_wg = jnp.concatenate([jnp.concatenate(x[1][:3], 1) for x in halves], 0)
        pd_r = [jnp.concatenate(x[0][3:], 1) for x in halves]
        ds_r = [jnp.concatenate(x[1][3:], 1) for x in halves]
        att = dot(pd_wg, vwg) + jnp.concatenate([dot(a, b) for a, b in zip(pd_r, vr)], 0)
        att_v[at, :] = att.astype(bf)
        dq = dot(ds_wg, kwg) + jnp.concatenate([dot(a, b) for a, b in zip(ds_r, kr)], 0)
        dq_v[at, :] = (dq * SCALE).astype(bf)
        dk = dot_tn(ds_wg, q) * SCALE
        acck[h, ext, :] += dk[:4 * B]
        gacck[h] += dk[4 * B:]
        for half in range(2):
            dkr = dot_tn(ds_r[half], q[half * B:(half + 1) * B]) * SCALE
            store_terms(tk, h, p, half, dkr.astype(bf))
        return c

    def give_back(n, m, acc, gacc, term, stage):
        for h in range(HD):
            rim[n, 0, h] = acc[h, :B].astype(bf)
            rim[n, 1, h] = acc[h, B + T:].astype(bf)
            for c in range(4):
                gsum[n, h * 4 + c] = gacc[h, c * 32:(c + 1) * 32].astype(bf)
        near(acc, acc_out.at[n], local.at[2 + n])

        def gather(t):
            for j, off in enumerate(OFFS + ((0, 0),)):
                stage[j, t] = term[inverse[seq_peer(s, off), 0, t]]

        def send(t):
            for j, off in enumerate(OFFS):
                remote(
                    stage.at[j, t], ret_out.at[n, s, t], send_r.at[m], recv_r.at[m],
                    seq_peer(s, off),
                )
            near(stage.at[NS - 1, t], ret_out.at[n, s, t], recv_r.at[m])

        for e in range(EXTRA):
            back[n, e] = term[extra_s[1 + e]]
        gather(0)
        for e in range(EXTRA):
            a, b, _, _, shard = axes(e)
            for to in ring(b):
                remote(
                    back.at[n, e], back_in.at[n, e, b], ex_s.at[2 * m], ex_r.at[2 * m],
                    shard(a, to),
                )
            near(back.at[n, e], back_in.at[n, e, b], ex_r.at[2 * m])
        everyone(lambda p: gsum.at[n, p], gpart.at[n, s], gl_s.at[2 * m], gl_r.at[2 * m])
        remote(rim.at[n, 0], rim_out.at[n, 1], rim_s.at[n], rim_r.at[n], prv)
        remote(rim.at[n, 1], rim_out.at[n, 0], rim_s.at[n], rim_r.at[n], nxt)
        for t in range(CAP):
            if t + 1 < CAP:
                gather(t + 1)
            send(t)
            if t == 5:
                drain(gpart.at[n], gl_r.at[2 * m])
                total = gpart[n, 0].astype(f32)
                for i in range(1, NS):
                    total = total + gpart[n, i].astype(f32)
                gdone[n] = total.astype(bf)
                drain(back_in.at[n], ex_r.at[2 * m])
                for e in range(EXTRA):
                    a, b, _, _, shard = axes(e)
                    for to in ring(a):
                        remote(
                            back_in.at[n, e], more_out.at[n, e, a], ex_s.at[2 * m + 1],
                            ex_r.at[2 * m + 1], shard(to, b),
                        )
                    near(back_in.at[n, e], more_out.at[n, e, a], ex_r.at[2 * m + 1])
            if t == 6:
                everyone(
                    lambda p: gdone.at[n], gtot_out.at[n, s], gl_s.at[2 * m + 1],
                    gl_r.at[2 * m + 1],
                )

    lax.fori_loop(0, HD * NB // 2, phase1, 0)
    drain(sk.at[tail], send_r.at[0])
    give_back(1, 2, accv, gaccv, tv, sk)
    await_blocks(1, values, rv)
    lax.fori_loop(0, HD * NB // 2, phase2, 0)
    drain(sv.at[tail], send_r.at[1])
    give_back(0, 3, acck, gacck, tk, sv)
    for h in range(HD):
        near(att_v.at[pl.ds(h * T, T), :], att_out.at[:, pl.ds(h * W, W)], local.at[4])
        near(dq_v.at[pl.ds(h * T, T), :], dq_out.at[:, pl.ds(h * W, W)], local.at[5])

    drain(wanted_v, local.at[1])
    drain(wanted_v.at[tail], send_t)
    drain(probs.at[pl.ds(0, 28), :, pl.ds(0, 256)], send_x)
    for n in range(2):
        drain(kh, halo_s.at[n])
        drain(rim.at[n], rim_s.at[n])
        drain(rim_out.at[n], rim_r.at[n])
        drain((acck, accv)[n], local.at[2 + n])
    for m in range(8):
        drain(glob.at[0, tail], gl_s.at[m])
    for n in range(2):
        step1 = first.at[n, :, pl.ds(0, 3)]
        step2 = second.at[n, :, pl.ds(0, 3)]
        drain(step1, ex_s.at[2 * n])
        drain(step2, ex_s.at[2 * n + 1])
        drain(step2, ex_s.at[4 + 2 * n])
        drain(step1, ex_s.at[5 + 2 * n])
        drain(more_out.at[n], ex_r.at[7 - 2 * n])
    drain(gtot_out.at[1], gl_r.at[5])
    drain(gtot_out.at[0], gl_r.at[7])
    drain(att_v, local.at[4])
    drain(dq_v, local.at[5])
    drain(sk.at[tail], send_r.at[2])
    drain(ret_out.at[1], recv_r.at[2])
    drain(sv.at[tail], send_r.at[3])
    drain(ret_out.at[0], recv_r.at[3])


def main_call(q, k, v, g, table, inverse, slots, extra, drops, gids):
    bf, f32 = jnp.bfloat16, jnp.float32
    sds = jax.ShapeDtypeStruct
    dma = pltpu.SemaphoreType.DMA
    sm = spec(pltpu.SMEM)
    tile = (B, W)
    chunk = (NS, 32, W)
    return pl.pallas_call(
        main_kernel,
        name="exchange_attend",
        out_shape=(
            sds((T, HD * W), bf), sds((T, HD * W), bf), sds((2, HD, EB * B, W), f32),
            sds((2, NS, CAP) + tile, bf), sds((2, EXTRA, 4, 4) + tile, bf), sds((2, 2, HD) + tile, bf), sds((2,) + chunk, bf),
            sds((NS, 1, 128), jnp.int32),
        ),
        in_specs=[spec(ANY)] * 5 + [sm] * 5,
        out_specs=(spec(ANY),) * 8,
        scratch_shapes=[
            VM((HD * EB, CUT, W), bf), VM((HD * EB, B - CUT, W), bf), VM((HD * EB,) + tile, bf),
            VM((HD * T, W), bf), VM((HD * T, W), bf),
            VM((2, HD) + tile, bf), VM((2, HD) + tile, bf),
            VM((NS, CAP) + tile, bf), VM((NS, CAP) + tile, bf),
            VM((NS * CAP + EXTRA,) + tile, bf), VM((NS * CAP + EXTRA,) + tile, bf),
            VM((HD * NB // 2, 2 * B, 640), f32),
            VM((REQ,) + tile, bf), VM((REQ,) + tile, bf),
            VM((HD, EB * B, W), f32), VM((HD, EB * B, W), f32),
            VM((HD, 2 * B, W), f32), VM((HD, 2 * B, W), f32),
            VM((HD * T, W), bf), VM((HD * T, W), bf),
            VM((NS, 1, 128), jnp.int32), pltpu.SMEM((NS, 1, 128), jnp.int32),
            VM((2,) + chunk, bf), VM(chunk, bf), VM(chunk, bf), VM((2, 32, W), bf), VM((2,) + chunk, bf),
            VM((2,) + chunk, bf), VM((2,) + chunk, bf), VM((2, 32, W), bf),
            VM((2, 2, HD) + tile, bf),
            VM((2, EXTRA, 4, 4) + tile, bf), VM((EXTRA * 16,) + tile, bf), VM((EXTRA * 16,) + tile, bf),
            VM((2, EXTRA, 4) + tile, bf), VM((EXTRA * 4,) + tile, bf), VM((EXTRA * 4,) + tile, bf),
            VM((2, EXTRA) + tile, bf), VM((2, EXTRA, 4) + tile, bf),
            dma, dma((5,)), dma, dma, dma((6,)), dma((4,)), dma((4,)),
            dma((2,)), dma((2,)), dma((8,)), dma((8,)), dma((2,)), dma((2,)), dma((8,)), dma((8,)),
        ],
        compiler_params=pltpu.CompilerParams(
            collective_id=0, has_side_effects=True, vmem_limit_bytes=VLIM
        ),
    )(q, k, v, g, table, inverse, slots, extra, drops, gids)


def gather_up_kernel(
    wanted, gids, shard, extra, acc_in, rim, gtot, ret, more, att_in, dq_in, dk_ref, dv_ref, att_ref, dq_ref, acc
):
    s = shard[0]
    i = pl.program_id(0)
    f32 = jnp.float32
    att_ref[...] = att_in[...]
    dq_ref[...] = dq_in[...]
    for h in range(HD):
        for b in range(NB):
            at = slice((b + 1) * B, (b + 2) * B)
            acc[h * EB + 1 + b] = acc_in[0, h, at]

        @pl.when(s > 0)
        def _():
            acc[h * EB + 1] += rim[0, 0, h].astype(f32)

        @pl.when(s < NS - 1)
        def _():
            acc[h * EB + NB] += rim[0, 1, h].astype(f32)

        for gb in range(G):
            mine = gids[gb] - s * NB

            @pl.when(jnp.logical_and(mine >= 0, mine < NB))
            def _():
                acc[h * EB + 1 + mine] += gtot[0, pl.ds(h * 4 + gb * 2, 2)].reshape(B, W).astype(f32)

    def add(lister, c):
        for t in range(CAP):
            code = wanted[lister, 0, t]
            at = jnp.where(code < 0, HD * EB, code)
            acc[at] += ret[0, lister, t].astype(f32)
        return c

    lax.fori_loop(0, NS, add, 0)

    @pl.when(s == extra[0])
    def _():
        for e in range(EXTRA):
            for a in range(4):
                for b in range(4):
                    code = wanted[b * 4 + a if e == 0 else a * 4 + b, 0, CAP + e]
                    at = jnp.where(code < 0, HD * EB, code)
                    acc[at] += more[0, e, a, b].astype(f32)

    for n, out in enumerate((dk_ref, dv_ref)):

        @pl.when(i == n)
        def _():
            for h in range(HD):
                for b in range(NB):
                    out[b * B:(b + 1) * B, h * W:(h + 1) * W] = acc[h * EB + 1 + b].astype(jnp.bfloat16)


def gather_up(wanted, gids, shard, extra, acc, rim, gtot, ret, more, att, dq):
    sds = jax.ShapeDtypeStruct
    sm = spec(pltpu.SMEM)
    whole = pl.BlockSpec((T, HD * W), lambda i: (0, 0))
    part = pl.BlockSpec((T // 2, HD * W), lambda i: (i, 0))
    return pl.pallas_call(
        gather_up_kernel,
        name="gather_up",
        grid=(2,),
        out_shape=(sds((T, HD * W), jnp.bfloat16),) * 4,
        in_specs=[
            sm, sm, sm, sm,
            pl.BlockSpec((1, HD, EB * B, W), lambda i: (i, 0, 0, 0)),
            pl.BlockSpec((1, 2, HD, B, W), lambda i: (i, 0, 0, 0, 0)),
            pl.BlockSpec((1, NS, 32, W), lambda i: (i, 0, 0, 0)),
            pl.BlockSpec((1, NS, CAP, B, W), lambda i: (i, 0, 0, 0, 0)),
            pl.BlockSpec((1, EXTRA, 4, 4, B, W), lambda i: (i, 0, 0, 0, 0, 0)),
            part, part,
        ],
        out_specs=(whole, whole, part, part),
        scratch_shapes=[VM((HD * EB + 1, B, W), jnp.float32)],
        compiler_params=pltpu.CompilerParams(vmem_limit_bytes=VLIM),
    )(wanted, gids, shard, extra, acc, rim, gtot, ret, more, att, dq)


def per_device(queries, keys, values, grad_out, rand_blocks, global_ids, drop_mask):
    shard = lax.axis_index("seq").astype(jnp.int32).reshape(1)
    table, inverse, slots, extra = request_table(rand_blocks.transpose(2, 0, 1))
    att, dq, acc, ret, more, rim, gtot, wanted = main_call(
        queries, keys, values, grad_out, table, inverse, slots, extra,
        drop_mask.transpose(0, 2, 1), global_ids,
    )
    dk, dv, att, dq = gather_up(
        wanted, global_ids, shard, extra, acc, rim, gtot, ret, more, att, dq
    )
    return att, dq, dk, dv


def solution(mesh):
    rows = P(("seq", "head"), None)
    out = P("seq", "head")
    return jax.shard_map(
        per_device,
        mesh=mesh,
        in_specs=(rows, rows, rows, rows, P("head", "seq", None), P(), P("head", "seq", None)),
        out_specs=(out, out, out, out),
        check_vma=False,
    )
```
